32 devices in a mesh: frame: 4 (over y, x), row: 8 (over z, core).
Axes of the slice: x: 2, y: 2, z: 4, core: 2. Of those that a mesh axis runs over, the one named last changes fastest.
Arguments:
- frames_in: bfloat16 [8, 32, 32, 256], P('frame', 'row'), may hold values from -6 to 6
- conv_first: bfloat16 [3, 3, 256, 256], replicated, may hold values from -0.125 to 0.125
- conv_second: bfloat16 [3, 3, 256, 256], replicated, may hold values from -0.125 to 0.125
- time_kernel: bfloat16 [3, 256, 256], replicated, may hold values from -0.21875 to 0.21875
- norm_gain: float32 [256], replicated, may hold values from 0.1 to 1.9
- w_query: bfloat16 [256, 256], replicated, may hold values from -0.375 to 0.375
- w_key: bfloat16 [256, 256], replicated, may hold values from -0.375 to 0.375
- w_value: bfloat16 [256, 256], replicated, may hold values from -0.375 to 0.375
- w_out: bfloat16 [256, 256], replicated, may hold values from -0.375 to 0.375
- frame_bias: float32 [8, 8], replicated, may hold values from -6 to 400
- conv_third: bfloat16 [3, 3, 256, 256], replicated, may hold values from -0.125 to 0.125
Outputs:
- encoded: bfloat16 [8, 32, 32, 256], P(None, 'row', 'frame')
The draws below stay inside these ranges and needn't reach their ends.
All inputs are finite; a program needn't handle non-finite values.
Results may differ from the reference program's by a relative error of at most 0.018.
Values may be sent and summed in bfloat16 or wider, within the bound.
A program may use at most 64 MiB of HBM per device.

```python
import math
import jax
import jax.numpy as jnp
from jax import lax

C = 256
FRAMES = 8
HEIGHT = 32
WIDTH = 32


def draw_frame_bias(key, part):
    drawn = jnp.clip(jax.random.normal(key, (FRAMES, FRAMES), jnp.float32), -6.0, 6.0)
    return drawn


def level_of(key, shape, pieces, low, largest):
    loudness = 1.0
    for dim, parts in pieces:
        draws = jax.random.uniform(jax.random.fold_in(jax.random.fold_in(key, 6), dim), (parts,), jnp.float32, low / len(pieces), largest / len(pieces))
        loudness = loudness * jnp.repeat(jnp.exp(draws), shape[dim] // parts).reshape((-1,) + (1,) * (len(shape) - 1 - dim))
    return loudness


def scatter_about(key, dims, deviation, reach, split=(), held_as=jnp.bfloat16):
    values = deviation * jax.random.normal(key, dims, jnp.float32)
    if split:
        values = values * level_of(key, dims, split, -0.22, 0.18)
    return jnp.clip(values, -reach, reach).astype(held_as)


def setup_inputs(seed: int = 0) -> dict:
    arg_keys = jax.random.split(jax.random.key(seed), 12)
    frames_in = scatter_about(arg_keys[0], (FRAMES, HEIGHT, WIDTH, C), 1.0, 6.0, ((0, 4), (1, 8)))
    conv_first = scatter_about(arg_keys[1], (3, 3, C, C), (9 * C) ** -0.5, 0.125)
    conv_second = scatter_about(arg_keys[2], (3, 3, C, C), (9 * C) ** -0.5, 0.125)
    time_kernel = scatter_about(arg_keys[3], (3, C, C), (3 * C) ** -0.5, 0.21875)
    norm_gain = jnp.clip(1.0 + 0.18 * jax.random.normal(arg_keys[4], (C,), jnp.float32), 0.1, 1.9)
    w_query = scatter_about(arg_keys[5], (C, C), C ** -0.5, 0.375)
    w_key = scatter_about(arg_keys[6], (C, C), C ** -0.5, 0.375)
    w_value = scatter_about(arg_keys[7], (C, C), C ** -0.5, 0.375)
    w_out = scatter_about(arg_keys[8], (C, C), C ** -0.5, 0.375)
    frame_bias = draw_frame_bias(jax.random.fold_in(arg_keys[11], 71), 0)
    conv_third = scatter_about(arg_keys[10], (3, 3, C, C), (9 * C) ** -0.5, 0.125)
    return {"frames_in": frames_in, "conv_first": conv_first, "conv_second": conv_second, "time_kernel": time_kernel, "norm_gain": norm_gain, "w_query": w_query, "w_key": w_key, "w_value": w_value, "w_out": w_out, "frame_bias": frame_bias, "conv_third": conv_third}


def spatial(padded, weight, row_count, col_count):
    channels = weight.shape[2]
    summed = jnp.zeros((padded.shape[0] * row_count * col_count, weight.shape[3]), jnp.float32)
    for row_tap in range(3):
        for col_tap in range(3):
            window = padded[:, row_tap:row_tap + row_count, col_tap:col_tap + col_count, :]
            summed = summed + jnp.dot(window.reshape(-1, channels), weight[row_tap, col_tap], preferred_element_type=jnp.float32)
    return summed.reshape(padded.shape[0], row_count, col_count, weight.shape[3])

def pad_image(field):
    return jnp.pad(field, ((0, 0), (1, 1), (1, 1), (0, 0)))

def temporal(moved, time_kernel, norm_gain, w_query, w_key, w_value, w_out, frame_bias):
    frame_count = moved.shape[0]
    channels = moved.shape[-1]
    pixels = moved.reshape(frame_count, -1, channels)
    padded = jnp.pad(pixels, ((1, 1), (0, 0), (0, 0)))
    summed = pixels.astype(jnp.float32)
    for tap in range(3):
        shifted = padded[tap:tap + frame_count].reshape(-1, channels)
        summed = summed + jnp.dot(shifted, time_kernel[tap], preferred_element_type=jnp.float32).reshape(pixels.shape)
    timed = summed.astype(jnp.bfloat16)
    widened = timed.astype(jnp.float32)
    scale_inv = lax.rsqrt(lax.optimization_barrier(jnp.mean(widened * widened, axis=-1, keepdims=True)) + 1e-06)
    normed = (widened * scale_inv * norm_gain.astype(jnp.float32)).astype(jnp.bfloat16).reshape(-1, channels)
    queries = jnp.dot(normed, w_query, preferred_element_type=jnp.float32).astype(jnp.bfloat16).reshape(pixels.shape)
    key_rows = jnp.dot(normed, w_key, preferred_element_type=jnp.float32).astype(jnp.bfloat16).reshape(pixels.shape)
    value_rows = jnp.dot(normed, w_value, preferred_element_type=jnp.float32).astype(jnp.bfloat16).reshape(pixels.shape)
    scores = jnp.einsum('fpc,gpc->pfg', queries.astype(jnp.float32), key_rows.astype(jnp.float32)) / math.sqrt(channels)
    scores = scores + frame_bias.astype(jnp.float32)
    peak = lax.optimization_barrier(jnp.max(scores, axis=-1, keepdims=True))
    raised = jnp.exp(scores - peak)
    probs = (raised / lax.optimization_barrier(jnp.sum(raised, axis=-1, keepdims=True))).astype(jnp.bfloat16)
    context = jnp.einsum('pfg,gpc->fpc', probs.astype(jnp.float32), value_rows.astype(jnp.float32)).astype(jnp.bfloat16)
    projected = jnp.dot(context.reshape(-1, channels), w_out, preferred_element_type=jnp.float32).reshape(pixels.shape)
    return (widened + projected).astype(jnp.bfloat16).reshape(moved.shape)

def reference(frames_in, conv_first, conv_second, time_kernel, norm_gain, w_query, w_key, w_value, w_out, frame_bias, conv_third):
    row_count = frames_in.shape[1]
    col_count = frames_in.shape[2]
    first = jax.nn.silu(spatial(pad_image(frames_in), conv_first, row_count, col_count)).astype(jnp.bfloat16)
    second = jax.nn.silu(spatial(pad_image(first), conv_second, row_count, col_count)).astype(jnp.bfloat16)
    attended = temporal(second, time_kernel, norm_gain, w_query, w_key, w_value, w_out, frame_bias)
    return spatial(pad_image(attended), conv_third, row_count, col_count).astype(jnp.bfloat16)
```

```python
import functools
import math

import jax
import jax.numpy as jnp
from jax import lax
from jax.experimental import pallas as pl
from jax.experimental.pallas import tpu as pltpu
from jax.sharding import PartitionSpec as P

MESH = pl.DeviceIdType.MESH
BF16 = jnp.bfloat16
F32 = jnp.float32
HALO = 3
GROUP = 16


def matmul(lhs, rhs):
    return jnp.dot(lhs, rhs, preferred_element_type=F32)


def partner(index, distance, count):
    if count & (count - 1):
        return lax.rem(index + distance, count)
    bit = 1
    while bit < count:
        if distance & bit:
            index = index + bit - 2 * bit * lax.rem(lax.div(index, bit), 2)
        bit *= 2
    return index


def silu(v):
    half = 0.5 * v
    return half + half * jnp.tanh(half)


def silu_of_sum(one, two):
    half = 0.5 * one + 0.5 * two
    return half + half * jnp.tanh(half)


def steps_below(index, pitch, count):
    quotient = jnp.zeros_like(index)
    for k in range(1, count):
        quotient = quotient + (index >= k * pitch).astype(jnp.int32)
    return quotient


def shifted_columns(rows, width):
    count, _, channels = rows.shape
    flat = rows.astype(F32).reshape(count * width, channels)
    column = lax.broadcasted_iota(jnp.int32, (count, width, channels), 1)
    left = pltpu.roll(flat, 1, 0).reshape(count, width, channels)
    right = pltpu.roll(flat, count * width - 1, 0).reshape(count, width, channels)
    left = jnp.where(column == 0, 0.0, left).astype(BF16)
    right = jnp.where(column == width - 1, 0.0, right).astype(BF16)
    return left, right


def spread(dst, first_row, rows, width):
    count, _, channels = rows.shape
    left, right = shifted_columns(rows, width)
    span = slice(first_row, first_row + count)
    dst[span, :, 0:channels] = left
    dst[span, :, channels : 2 * channels] = rows
    dst[span, :, 2 * channels : 3 * channels] = right


def kernel(
    frames_axis,
    rows_axis,
    x_hbm,
    w1_hbm,
    w2_hbm,
    tk_hbm,
    gain_hbm,
    wq_hbm,
    wk_hbm,
    wv_hbm,
    wo_hbm,
    bias_hbm,
    w3_hbm,
    out_ref,
    xin,
    far_in,
    near_in,
    xs,
    fs,
    w1,
    w2,
    tk,
    wq,
    wk,
    wv,
    wo,
    w3,
    partial,
    gain_ref,
    bias_ref,
    packed,
    moved,
    context,
    cols3,
    load_sem,
    halo_send,
    halo_recv,
    send_sem,
    recv_sem,
):
    frame = lax.axis_index("frame")
    row = lax.axis_index("row")
    local_frames, n, width, channels = x_hbm.shape
    frame_count = frames_axis * local_frames
    cols = width // frames_axis
    half_rows = (n + 2) // 2
    slots = packed.shape[3]

    odd = lax.rem(row, 2)
    near = row + 1 - 2 * odd
    far = lax.rem(row - 1 + 2 * odd + rows_axis, rows_axis)
    has_far = (row + odd > 0) & (row + odd < rows_axis)

    barrier = pltpu.get_barrier_semaphore()

    @pl.when(has_far)
    def _():
        pl.semaphore_signal(barrier, inc=1, device_id={"row": far}, device_id_type=MESH)

    pl.semaphore_signal(barrier, inc=1, device_id={"row": near}, device_id_type=MESH)
    for k in range(1, frames_axis):
        peer = lax.rem(frame + k, frames_axis)
        pl.semaphore_signal(barrier, inc=1, device_id={"frame": peer}, device_id_type=MESH)

    count = [0]

    def load(src, dst):
        copy = pltpu.make_async_copy(src, dst, load_sem.at[count[0]])
        count[0] += 1
        copy.start()
        return copy

    def mirrored(i, size):
        return i + odd * (size - 1 - 2 * i)

    x_loads = [load(x_hbm.at[:, i], xin.at[:, mirrored(i, n)]) for i in range(n)]
    w1_loads = [load(w1_hbm.at[a], w1.at[mirrored(a, 3)]) for a in range(3)]
    w2_loads = [load(w2_hbm.at[a], w2.at[mirrored(a, 3)]) for a in range(3)]
    late_loads = [
        load(src, dst)
        for src, dst in (
            (tk_hbm, tk),
            (gain_hbm, gain_ref),
            (wq_hbm, wq),
            (wk_hbm, wk),
            (wv_hbm, wv),
            (bias_hbm, bias_ref),
            (wo_hbm, wo),
        )
    ]
    w3_loads = [load(w3_hbm.at[a], w3.at[mirrored(a, 3)]) for a in range(3)]

    pl.semaphore_wait(barrier, has_far.astype(jnp.int32) + frames_axis)

    to_far = pltpu.make_async_remote_copy(
        src_ref=xin.at[:, 0:HALO],
        dst_ref=far_in,
        send_sem=halo_send.at[0],
        recv_sem=halo_recv.at[0],
        device_id={"row": far},
        device_id_type=MESH,
    )
    to_near = pltpu.make_async_remote_copy(
        src_ref=xin.at[:, n - HALO : n],
        dst_ref=near_in,
        send_sem=halo_send.at[1],
        recv_sem=halo_recv.at[1],
        device_id={"row": near},
        device_id_type=MESH,
    )
    for copy in x_loads:
        copy.wait()
    pl.when(has_far)(to_far.start)
    to_near.start()

    @pl.when(jnp.logical_not(has_far))
    def _():
        far_in[...] = jnp.zeros_like(far_in)

    shape = (frames_axis * slots, half_rows * width)
    target = lax.broadcasted_iota(jnp.int32, shape, 0)
    source = lax.broadcasted_iota(jnp.int32, shape, 1)
    owner = steps_below(target, slots, frames_axis)
    slot = target - owner * slots
    inner = half_rows * cols
    slot_row = steps_below(slot, cols, half_rows)
    slot_col = slot - slot_row * cols
    side = (slot >= inner + half_rows).astype(jnp.int32)
    outer = slot >= inner
    slot_row = jnp.where(outer, slot - inner - side * half_rows, slot_row)
    slot_col = jnp.where(outer, side * (cols + 1) - 1, slot_col) + owner * cols
    taken = (
        (slot < half_rows * (cols + 2))
        & (slot_col >= 0)
        & (slot_col < width)
        & (source == slot_row * width + slot_col)
    )
    pick = jnp.where(taken, 1.0, 0.0).astype(BF16)
    edge = jnp.zeros((2, 1, slots, channels), BF16)
    moved[:, 0:1] = edge
    moved[:, frame_count + 1 : frame_count + 2] = edge

    for f in range(local_frames):
        spread(xs.at[f], HALO, xin[f], width)
    for copy in w1_loads:
        copy.wait()
    own_rows = xs[:, HALO : HALO + n].reshape(-1, 3 * channels)
    shares = [
        matmul(own_rows, w1[a].reshape(3 * channels, channels)).reshape(
            local_frames, n, width, channels
        )
        for a in range(3)
    ]
    partial[:, 0] = shares[2][:, 0]
    partial[:, 1] = shares[1][:, 0] + shares[2][:, 1]
    partial[:, 2] = shares[0][:, n - 2] + shares[1][:, n - 1]
    partial[:, 3] = shares[0][:, n - 1]
    for f in range(local_frames):
        whole = [
            shares[0][f, t - 1] + shares[1][f, t] + shares[2][f, t + 1] for t in range(1, n - 1)
        ]
        spread(fs.at[f], 3, silu(jnp.stack(whole)).astype(BF16), width)

    def edges(rows, a):
        part = matmul(
            rows.reshape(-1, 3 * channels), w1[a].reshape(3 * channels, channels)
        )
        return part.reshape(local_frames, -1, width, channels)

    def second_half(half, first_row):
        def rows(a, k):
            taken = fs[:, first_row + a : first_row + a + half_rows, :, k : k + channels]
            return taken.reshape(-1, channels)

        taps = [(a, k * channels) for a in range(3) for k in range(3)]
        cut = (len(taps) + 1) // 2
        sums = []
        for some in (taps[:cut], taps[cut:]):
            total = None
            for a, k in some:
                part = matmul(rows(a, k), w2[a].reshape(3 * channels, channels)[k : k + channels])
                total = part if total is None else total + part
            sums.append(total)
        second = silu_of_sum(*sums).reshape(local_frames, half_rows, width, channels)
        if half == 0:
            place = lax.broadcasted_iota(jnp.int32, second.shape, 1)
            second = jnp.where((place > 0) | has_far, second, 0.0)
        second = second.astype(BF16).reshape(local_frames, half_rows * width, channels)
        for f in range(local_frames):
            packed[half, :, f] = (
                matmul(pick, second[f]).astype(BF16).reshape(frames_axis, slots, channels)
            )
        copies = []
        place = pl.ds(1 + frame * local_frames, local_frames)
        for k in reversed(range(1, frames_axis)):
            peer = partner(frame, k, frames_axis)
            copy = pltpu.make_async_remote_copy(
                src_ref=packed.at[half, peer],
                dst_ref=moved.at[half, place],
                send_sem=send_sem.at[half, k],
                recv_sem=recv_sem.at[half, k],
                device_id={"frame": peer},
                device_id_type=MESH,
            )
            copy.start()
            copies.append(copy)
        moved[half, place] = packed[half, frame]
        return copies

    to_near.wait_recv()
    for f in range(local_frames):
        spread(
            xs.at[f],
            HALO + n,
            jnp.stack([near_in[f, HALO - 1 - j] for j in range(HALO)]),
            width,
        )
    top = HALO + n
    two = edges(xs[:, top : top + 3], 2)
    one = edges(xs[:, top : top + 2], 1)
    zero = edges(xs[:, top : top + 1], 0)
    for f in range(local_frames):
        rows = jnp.stack(
            [
                partial[f, 2] + two[f, 0],
                partial[f, 3] + two[f, 1] + one[f, 0],
                two[f, 2] + one[f, 1] + zero[f, 0],
            ]
        )
        spread(fs.at[f], n + 1, silu(rows).astype(BF16), width)
    for copy in w2_loads:
        copy.wait()
    near_copies = second_half(1, half_rows)

    pl.when(has_far)(to_far.wait_recv)
    for f in range(local_frames):
        spread(
            xs.at[f], 0, jnp.stack([far_in[f, HALO - 1 - j] for j in range(HALO)]), width
        )
    zero = edges(xs[:, 0:3], 0)
    one = edges(xs[:, 1:3], 1)
    two = edges(xs[:, 2:3], 2)
    for f in range(local_frames):
        rows = jnp.stack(
            [
                zero[f, 0] + one[f, 0] + two[f, 0],
                partial[f, 0] + zero[f, 1] + one[f, 1],
                partial[f, 1] + zero[f, 2],
            ]
        )
        rows = silu(rows)
        place = lax.broadcasted_iota(jnp.int32, rows.shape, 0)
        rows = jnp.where((place > 1) | has_far, rows, 0.0)
        spread(fs.at[f], 0, rows.astype(BF16), width)
    far_copies = second_half(0, 0)

    for copy in late_loads:
        copy.wait()
    span = frame_count * GROUP
    lane = lax.broadcasted_iota(jnp.int32, (frame_count, span), 1)
    wide = jnp.zeros((frame_count, span), F32)
    for g in range(frame_count):
        inside = (lane >= g * GROUP) & (lane < (g + 1) * GROUP)
        wide = jnp.where(inside, bias_ref[:, g : g + 1], wide)
    wide = jnp.broadcast_to(wide[:, None, :], (frame_count, GROUP, span)).reshape(span, span)
    query_pixel = jnp.bitwise_and(lax.broadcasted_iota(jnp.int32, (span, span), 0), GROUP - 1)
    key_pixel = jnp.bitwise_and(lax.broadcasted_iota(jnp.int32, (span, span), 1), GROUP - 1)
    masked_bias = jnp.where(query_pixel == key_pixel, wide, -1e30)

    target = lax.broadcasted_iota(jnp.int32, (2 * inner, slots), 0)
    source = lax.broadcasted_iota(jnp.int32, (2 * inner, slots), 1)
    shift = (target >= inner).astype(jnp.int32)
    place = target - shift * inner
    place_row = steps_below(place, cols, half_rows)
    place_col = place - place_row * cols
    outer = place_col == shift * (cols - 1)
    wanted = jnp.where(outer, inner + shift * half_rows + place_row, place + 2 * shift - 1)
    pick3 = jnp.where(source == wanted, 1.0, 0.0).astype(BF16)

    pixels = frame_count * slots
    tile = (frame_count, slots, channels)

    def attend(half, copies, cols_row):
        for copy in copies:
            copy.wait_recv()
        here = moved.at[half]
        taps = [
            matmul(here[tap : tap + frame_count].reshape(pixels, channels), tk[tap])
            for tap in range(3)
        ]
        centre = here[1 : 1 + frame_count].reshape(pixels, channels).astype(F32)
        timed = (centre + taps[0] + taps[1] + taps[2]).astype(BF16)
        widened = timed.astype(F32)
        scale_inv = lax.rsqrt(jnp.mean(widened * widened, axis=-1, keepdims=True) + 1e-06)
        gained = (widened * gain_ref[...]).astype(BF16)
        queries = (matmul(gained, wq[...]) * scale_inv).astype(BF16).reshape(tile)
        key_rows = (matmul(gained, wk[...]) * scale_inv).astype(BF16).reshape(tile)
        value_rows = (matmul(gained, wv[...]) * scale_inv).astype(BF16).reshape(tile)
        groups = [slice(g * GROUP, (g + 1) * GROUP) for g in range(slots // GROUP)]
        scores = [
            lax.dot_general(
                queries[:, part].reshape(span, channels),
                key_rows[:, part].reshape(span, channels),
                (((1,), (1,)), ((), ())),
                preferred_element_type=F32,
            )
            for part in groups
        ]
        scores = [score * (1.0 / math.sqrt(channels)) + masked_bias for score in scores]
        peaks = [jnp.max(score, axis=-1, keepdims=True) for score in scores]
        raised = [jnp.exp(score - peak) for score, peak in zip(scores, peaks)]
        totals = [jnp.sum(r, axis=-1, keepdims=True) for r in raised]
        probs = [(r / total).astype(BF16) for r, total in zip(raised, totals)]
        for part, prob in zip(groups, probs):
            mixed = matmul(prob, value_rows[:, part].reshape(span, channels))
            context[half, :, part] = mixed.astype(BF16).reshape(frame_count, GROUP, channels)
        attended = widened + matmul(context[half].reshape(pixels, channels), wo[...])
        rounded = attended.astype(BF16).reshape(tile)
        attended = attended.reshape(tile)
        gathered = [matmul(pick3, rounded[f]) for f in range(frame_count)]
        for j in range(half_rows):
            at = slice(j * cols, (j + 1) * cols)
            past = slice(inner + j * cols, inner + (j + 1) * cols)
            frames = range(frame_count)
            for b, parts in enumerate(
                (
                    [gathered[f][at] for f in frames],
                    [attended[f, at] for f in frames],
                    [gathered[f][past] for f in frames],
                )
            ):
                cols3[cols_row + j, :, b * channels : (b + 1) * channels] = jnp.concatenate(
                    parts, axis=0
                ).astype(BF16)

    attend(1, near_copies, half_rows)
    attend(0, far_copies, 0)

    for copy in w3_loads:
        copy.wait()
    taps = [(a, k * channels) for a in range(3) for k in range(3)]
    cut = (len(taps) + 1) // 2
    summed = None
    for a, k in taps:
        part = matmul(
            cols3[a : a + n, :, k : k + channels].reshape(-1, channels),
            w3[a].reshape(3 * channels, channels)[k : k + channels],
        )
        summed = part if summed is None else summed + part
    summed = summed.reshape(n, frame_count, cols, channels)
    for t in range(n):
        out_ref[:, mirrored(t, n)] = summed[t].astype(BF16)

    pl.when(has_far)(to_far.wait_send)
    to_near.wait_send()
    for copy in near_copies + far_copies:
        copy.wait_send()


def on_device(frames_axis, rows_axis, *args):
    frames_in = args[0]
    norm_gain = args[4]
    local_frames, n, width, channels = frames_in.shape
    frame_count = local_frames * frames_axis
    cols = width // frames_axis
    half_rows = (n + 2) // 2
    slots = -(-half_rows * (cols + 2) // GROUP) * GROUP
    args = args[:4] + (norm_gain.reshape(1, channels),) + args[5:]
    any_space = pl.BlockSpec(memory_space=pl.ANY)
    vmem = pl.BlockSpec(memory_space=pltpu.VMEM)
    weight = pltpu.VMEM((3, 3, channels, channels), BF16)
    square = pltpu.VMEM((channels, channels), BF16)
    halo = pltpu.VMEM((local_frames, HALO, width, channels), BF16)
    return pl.pallas_call(
        functools.partial(kernel, frames_axis, rows_axis),
        out_shape=pltpu.VMEM((frame_count, n, cols, channels), BF16),
        in_specs=[any_space] * 11,
        out_specs=vmem,
        scratch_shapes=[
            pltpu.VMEM((local_frames, n, width, channels), BF16),
            halo,
            halo,
            pltpu.VMEM((local_frames, n + 2 * HALO, width, 3 * channels), BF16),
            pltpu.VMEM((local_frames, n + 4, width, 3 * channels), BF16),
            weight,
            weight,
            pltpu.VMEM((3, channels, channels), BF16),
            square,
            square,
            square,
            square,
            weight,
            pltpu.VMEM((local_frames, 4, width, channels), F32),
            pltpu.VMEM((1, channels), F32),
            pltpu.VMEM((frame_count, frame_count), F32),
            pltpu.VMEM((2, frames_axis, local_frames, slots, channels), BF16),
            pltpu.VMEM((2, frame_count + 2, slots, channels), BF16),
            pltpu.VMEM((2, frame_count, slots, channels), BF16),
            pltpu.VMEM((n + 2, frame_count * cols, 3 * channels), BF16),
            pltpu.SemaphoreType.DMA((n + 16,)),
            pltpu.SemaphoreType.DMA((2,)),
            pltpu.SemaphoreType.DMA((2,)),
            pltpu.SemaphoreType.DMA((2, frames_axis)),
            pltpu.SemaphoreType.DMA((2, frames_axis)),
        ],
        compiler_params=pltpu.CompilerParams(
            collective_id=0, has_side_effects=True, vmem_limit_bytes=56 * 1024 * 1024
        ),
    )(*args)


def solution(mesh):
    placed = (P("frame", "row", None, None),) + (P(),) * 10
    return jax.shard_map(
        functools.partial(on_device, mesh.shape["frame"], mesh.shape["row"]),
        mesh=mesh,
        in_specs=placed,
        out_specs=P(None, "row", "frame", None),
        check_vma=False,
    )
```

```python
import functools
import math

import jax
import jax.numpy as jnp
from jax import lax
from jax.experimental import pallas as pl
from jax.experimental.pallas import tpu as pltpu
from jax.sharding import PartitionSpec as P

MESH = pl.DeviceIdType.MESH
BF16 = jnp.bfloat16
F32 = jnp.float32
HALO = 3
GROUP = 16


def matmul(lhs, rhs):
    return jnp.dot(lhs, rhs, preferred_element_type=F32)


def partner(index, distance, count):
    if count & (count - 1):
        return lax.rem(index + distance, count)
    bit = 1
    while bit < count:
        if distance & bit:
            index = index + bit - 2 * bit * lax.rem(lax.div(index, bit), 2)
        bit *= 2
    return index


def silu(v):
    half = 0.5 * v
    return half + half * jnp.tanh(half)


def silu_of_sum(one, two):
    half = 0.5 * one + 0.5 * two
    return half + half * jnp.tanh(half)


def steps_below(index, pitch, count):
    quotient = jnp.zeros_like(index)
    for k in range(1, count):
        quotient = quotient + (index >= k * pitch).astype(jnp.int32)
    return quotient


def shifted_columns(rows, width):
    count, _, channels = rows.shape
    flat = rows.astype(F32).reshape(count * width, channels)
    column = lax.broadcasted_iota(jnp.int32, (count, width, channels), 1)
    left = pltpu.roll(flat, 1, 0).reshape(count, width, channels)
    right = pltpu.roll(flat, count * width - 1, 0).reshape(count, width, channels)
    left = jnp.where(column == 0, 0.0, left).astype(BF16)
    right = jnp.where(column == width - 1, 0.0, right).astype(BF16)
    return left, right


def spread(dst, first_row, rows, width):
    count, _, channels = rows.shape
    left, right = shifted_columns(rows, width)
    span = slice(first_row, first_row + count)
    dst[span, :, 0:channels] = left
    dst[span, :, channels : 2 * channels] = rows
    dst[span, :, 2 * channels : 3 * channels] = right


def kernel(
    frames_axis,
    rows_axis,
    x_hbm,
    w1_hbm,
    w2_hbm,
    tk_hbm,
    gain_hbm,
    wq_hbm,
    wk_hbm,
    wv_hbm,
    wo_hbm,
    bias_hbm,
    w3_hbm,
    out_ref,
    xin,
    far_in,
    near_in,
    xs,
    fs,
    w1,
    w2,
    tk,
    wq,
    wk,
    wv,
    wo,
    w3,
    partial,
    gain_ref,
    bias_ref,
    packed,
    moved,
    masked_bias,
    w_score,
    w_mixed,
    timed,
    normed,
    queries,
    values,
    cols3,
    load_sem,
    halo_send,
    halo_recv,
    send_sem,
    recv_sem,
):
    frame = lax.axis_index("frame")
    row = lax.axis_index("row")
    local_frames, n, width, channels = x_hbm.shape
    frame_count = frames_axis * local_frames
    cols = width // frames_axis
    half_rows = (n + 2) // 2
    slots = packed.shape[3]

    odd = lax.rem(row, 2)
    near = row + 1 - 2 * odd
    far = lax.rem(row - 1 + 2 * odd + rows_axis, rows_axis)
    has_far = (row + odd > 0) & (row + odd < rows_axis)

    once = 1 + lax.div(frame, frames_axis)

    def stage(body):
        lax.fori_loop(0, once, lambda _, carry: (body(), carry)[1], 0)

    barrier = pltpu.get_barrier_semaphore()

    @pl.when(has_far)
    def _():
        pl.semaphore_signal(barrier, inc=1, device_id={"row": far}, device_id_type=MESH)

    pl.semaphore_signal(barrier, inc=1, device_id={"row": near}, device_id_type=MESH)
    for k in range(1, frames_axis):
        peer = lax.rem(frame + k, frames_axis)
        pl.semaphore_signal(barrier, inc=1, device_id={"frame": peer}, device_id_type=MESH)

    count = [0]

    def load(src, dst):
        copy = pltpu.make_async_copy(src, dst, load_sem.at[count[0]])
        count[0] += 1
        copy.start()
        return copy

    def mirrored(i, size):
        return i + odd * (size - 1 - 2 * i)

    x_loads = [load(x_hbm.at[:, i], xin.at[:, mirrored(i, n)]) for i in range(n)]
    w1_loads = [load(w1_hbm.at[a], w1.at[mirrored(a, 3)]) for a in range(3)]
    w2_loads = [load(w2_hbm.at[a], w2.at[mirrored(a, 3)]) for a in range(3)]
    late_loads = [
        load(src, dst)
        for src, dst in (
            (tk_hbm, tk),
            (gain_hbm, gain_ref),
            (wq_hbm, wq),
            (wk_hbm, wk),
            (wv_hbm, wv),
            (bias_hbm, bias_ref),
            (wo_hbm, wo),
        )
    ]
    w3_loads = [load(w3_hbm.at[a], w3.at[mirrored(a, 3)]) for a in range(3)]

    pl.semaphore_wait(barrier, has_far.astype(jnp.int32) + frames_axis)

    to_far = pltpu.make_async_remote_copy(
        src_ref=xin.at[:, 0:HALO],
        dst_ref=far_in,
        send_sem=halo_send.at[0],
        recv_sem=halo_recv.at[0],
        device_id={"row": far},
        device_id_type=MESH,
    )
    to_near = pltpu.make_async_remote_copy(
        src_ref=xin.at[:, n - HALO : n],
        dst_ref=near_in,
        send_sem=halo_send.at[1],
        recv_sem=halo_recv.at[1],
        device_id={"row": near},
        device_id_type=MESH,
    )
    for copy in x_loads:
        copy.wait()
    pl.when(has_far)(to_far.start)
    to_near.start()

    @pl.when(jnp.logical_not(has_far))
    def _():
        far_in[...] = jnp.zeros_like(far_in)

    inner = half_rows * cols
    edge = jnp.zeros((2, 1, slots, channels), BF16)
    moved[:, 0:1] = edge
    moved[:, frame_count + 1 : frame_count + 2] = edge

    for f in range(local_frames):
        spread(xs.at[f], HALO, xin[f], width)
    for copy in w1_loads:
        copy.wait()
    @stage
    def _():
        own_rows = xs[:, HALO : HALO + n].reshape(-1, 3 * channels)
        shares = [
            matmul(own_rows, w1[a].reshape(3 * channels, channels)).reshape(
                local_frames, n, width, channels
            )
            for a in range(3)
        ]
        partial[:, 0] = shares[2][:, 0]
        partial[:, 1] = shares[1][:, 0] + shares[2][:, 1]
        partial[:, 2] = shares[0][:, n - 2] + shares[1][:, n - 1]
        partial[:, 3] = shares[0][:, n - 1]
        for f in range(local_frames):
            whole = [
                shares[0][f, t - 1] + shares[1][f, t] + shares[2][f, t + 1] for t in range(1, n - 1)
            ]
            spread(fs.at[f], 3, silu(jnp.stack(whole)).astype(BF16), width)

    def edges(rows, a):
        part = matmul(
            rows.reshape(-1, 3 * channels), w1[a].reshape(3 * channels, channels)
        )
        return part.reshape(local_frames, -1, width, channels)

    def pack(half, second):
        none = jnp.zeros((local_frames, cols, channels), F32)
        place = lax.broadcasted_iota(jnp.int32, none.shape, 1)
        blocks = [
            [second[:, j, o * cols : (o + 1) * cols] for j in range(half_rows)]
            for o in range(frames_axis)
        ]
        for o in range(frames_axis):
            outer = none
            for side, (p, at) in enumerate(((o - 1, cols - 1), (o + 1, 0))):
                if not 0 <= p < frames_axis:
                    continue
                for j in range(half_rows):
                    to = side * half_rows + j
                    turned = pltpu.roll(blocks[p][j], (to - at) % cols, 1)
                    outer = jnp.where(place == to, turned, outer)
            packed[half, o] = jnp.concatenate([*blocks[o], outer], axis=1).astype(BF16)

    def second_half(half, first_row):
        @stage
        def _():
            def rows(a, k):
                taken = fs[:, first_row + a : first_row + a + half_rows, :, k : k + channels]
                return taken.reshape(-1, channels)

            taps = [(a, k * channels) for a in range(3) for k in range(3)]
            cut = (len(taps) + 1) // 2
            sums = []
            for some in (taps[:cut], taps[cut:]):
                total = None
                for a, k in some:
                    part = matmul(rows(a, k), w2[a].reshape(3 * channels, channels)[k : k + channels])
                    total = part if total is None else total + part
                sums.append(total)
            second = silu_of_sum(*sums).reshape(local_frames, half_rows, width, channels)
            if half == 0:
                place = lax.broadcasted_iota(jnp.int32, second.shape, 1)
                second = jnp.where((place > 0) | has_far, second, 0.0)
            pack(half, second)

        copies = []
        place = pl.ds(1 + frame * local_frames, local_frames)
        for k in reversed(range(1, frames_axis)):
            peer = partner(frame, k, frames_axis)
            copy = pltpu.make_async_remote_copy(
                src_ref=packed.at[half, peer],
                dst_ref=moved.at[half, place],
                send_sem=send_sem.at[half, k],
                recv_sem=recv_sem.at[half, k],
                device_id={"frame": peer},
                device_id_type=MESH,
            )
            copy.start()
            copies.append(copy)
        moved[half, place] = packed[half, frame]
        return copies

    to_near.wait_recv()
    for f in range(local_frames):
        spread(
            xs.at[f],
            HALO + n,
            jnp.stack([near_in[f, HALO - 1 - j] for j in range(HALO)]),
            width,
        )
    @stage
    def _():
        top = HALO + n
        two = edges(xs[:, top : top + 3], 2)
        one = edges(xs[:, top : top + 2], 1)
        zero = edges(xs[:, top : top + 1], 0)
        for f in range(local_frames):
            rows = jnp.stack(
                [
                    partial[f, 2] + two[f, 0],
                    partial[f, 3] + two[f, 1] + one[f, 0],
                    two[f, 2] + one[f, 1] + zero[f, 0],
                ]
            )
            spread(fs.at[f], n + 1, silu(rows).astype(BF16), width)

    for copy in w2_loads:
        copy.wait()
    near_copies = second_half(1, half_rows)

    pl.when(has_far)(to_far.wait_recv)
    for f in range(local_frames):
        spread(
            xs.at[f], 0, jnp.stack([far_in[f, HALO - 1 - j] for j in range(HALO)]), width
        )
    @stage
    def _():
        zero = edges(xs[:, 0:3], 0)
        one = edges(xs[:, 1:3], 1)
        two = edges(xs[:, 2:3], 2)
        for f in range(local_frames):
            rows = jnp.stack(
                [
                    zero[f, 0] + one[f, 0] + two[f, 0],
                    partial[f, 0] + zero[f, 1] + one[f, 1],
                    partial[f, 1] + zero[f, 2],
                ]
            )
            rows = silu(rows)
            place = lax.broadcasted_iota(jnp.int32, rows.shape, 0)
            rows = jnp.where((place > 1) | has_far, rows, 0.0)
            spread(fs.at[f], 0, rows.astype(BF16), width)

    far_copies = second_half(0, 0)

    for copy in late_loads:
        copy.wait()
    span = frame_count * GROUP
    lane = lax.broadcasted_iota(jnp.int32, (frame_count, span), 1)
    wide = jnp.zeros((frame_count, span), F32)
    for g in range(frame_count):
        inside = (lane >= g * GROUP) & (lane < (g + 1) * GROUP)
        wide = jnp.where(inside, bias_ref[:, g : g + 1], wide)
    wide = jnp.broadcast_to(wide[:, None, :], (frame_count, GROUP, span)).reshape(span, span)
    query_pixel = jnp.bitwise_and(lax.broadcasted_iota(jnp.int32, (span, span), 0), GROUP - 1)
    key_pixel = jnp.bitwise_and(lax.broadcasted_iota(jnp.int32, (span, span), 1), GROUP - 1)
    masked_bias[...] = jnp.where(query_pixel == key_pixel, wide, -1e30)

    @stage
    def _():
        wide = lax.dot_general(
            wq[...], wk[...], (((1,), (1,)), ((), ())), preferred_element_type=F32
        )
        w_score[...] = (wide * (1.0 / math.sqrt(channels))).astype(BF16)
        w_mixed[...] = matmul(wv[...], wo[...]).astype(BF16)

    pixels = frame_count * slots
    tile = (frame_count, slots, channels)
    ones = jnp.ones((span, GROUP * 8), BF16)

    def attend(half, copies, cols_row):
        for copy in copies:
            copy.wait_recv()

        @stage
        def _():
            here = moved.at[half]
            taps = [
                matmul(here[tap : tap + frame_count].reshape(pixels, channels), tk[tap])
                for tap in range(3)
            ]
            centre = here[1 : 1 + frame_count].reshape(pixels, channels).astype(F32)
            rounded = (centre + taps[0] + taps[1] + taps[2]).astype(BF16)
            widened = rounded.astype(F32)
            scale_inv = lax.rsqrt(jnp.mean(widened * widened, axis=-1, keepdims=True) + 1e-06)
            timed[...] = rounded.reshape(tile)
            normed[...] = (widened * scale_inv * gain_ref[...]).astype(BF16).reshape(tile)

        @stage
        def _():
            rows = normed[...].reshape(pixels, channels)
            queries[...] = matmul(rows, w_score[...]).astype(BF16).reshape(tile)
            values[...] = matmul(rows, w_mixed[...]).astype(BF16).reshape(tile)

        @stage
        def _():
            groups = [slice(g * GROUP, (g + 1) * GROUP) for g in range(slots // GROUP)]
            scores = [
                lax.dot_general(
                    queries[:, part].reshape(span, channels),
                    normed[:, part].reshape(span, channels),
                    (((1,), (1,)), ((), ())),
                    preferred_element_type=F32,
                )
                for part in groups
            ]
            scores = [score + masked_bias[...] for score in scores]
            peaks = [jnp.max(score, axis=-1, keepdims=True) for score in scores]
            raised = [jnp.exp(score - peak).astype(BF16) for score, peak in zip(scores, peaks)]
            parts = []
            for part, r in zip(groups, raised):
                total = matmul(r, ones)[:, 0:1]
                mixed = matmul(r, values[:, part].reshape(span, channels)) / total
                parts.append(mixed.reshape(frame_count, GROUP, channels))
            attended = timed[...].astype(F32) + jnp.concatenate(parts, axis=1)
            outer = attended[:, inner : inner + cols]
            place = lax.broadcasted_iota(jnp.int32, outer.shape, 1)
            for j in range(half_rows):
                here = attended[:, j * cols : (j + 1) * cols]
                left = jnp.where(
                    place == 0, pltpu.roll(outer, -j % cols, 1), pltpu.roll(here, 1, 1)
                )
                right = jnp.where(
                    place == cols - 1,
                    pltpu.roll(outer, (cols - 1 - half_rows - j) % cols, 1),
                    pltpu.roll(here, cols - 1, 1),
                )
                for b, part in enumerate((left, here, right)):
                    cols3[cols_row + j, :, b * channels : (b + 1) * channels] = part.reshape(
                        frame_count * cols, channels
                    ).astype(BF16)

    attend(1, near_copies, half_rows)
    for copy in w3_loads:
        copy.wait()
    attend(0, far_copies, 0)

    @stage
    def _():
        taps = [(a, k * channels) for a in range(3) for k in range(3)]
        cut = (len(taps) + 1) // 2
        sums = []
        for some in (taps[:cut], taps[cut:]):
            total = None
            for a, k in some:
                part = matmul(
                    cols3[a : a + n, :, k : k + channels].reshape(-1, channels),
                    w3[a].reshape(3 * channels, channels)[k : k + channels],
                )
                total = part if total is None else total + part
            sums.append(total)
        summed = (sums[0] + sums[1]).reshape(n, frame_count, cols, channels)
        for t in range(n):
            out_ref[:, mirrored(t, n)] = summed[t].astype(BF16)

    pl.when(has_far)(to_far.wait_send)
    to_near.wait_send()
    for copy in near_copies + far_copies:
        copy.wait_send()


def on_device(frames_axis, rows_axis, *args):
    frames_in = args[0]
    norm_gain = args[4]
    local_frames, n, width, channels = frames_in.shape
    frame_count = local_frames * frames_axis
    cols = width // frames_axis
    half_rows = (n + 2) // 2
    slots = -(-half_rows * (cols + 2) // GROUP) * GROUP
    args = args[:4] + (norm_gain.reshape(1, channels),) + args[5:]
    any_space = pl.BlockSpec(memory_space=pl.ANY)
    vmem = pl.BlockSpec(memory_space=pltpu.VMEM)
    weight = pltpu.VMEM((3, 3, channels, channels), BF16)
    square = pltpu.VMEM((channels, channels), BF16)
    pixels = pltpu.VMEM((frame_count, slots, channels), BF16)
    halo = pltpu.VMEM((local_frames, HALO, width, channels), BF16)
    return pl.pallas_call(
        functools.partial(kernel, frames_axis, rows_axis),
        out_shape=pltpu.VMEM((frame_count, n, cols, channels), BF16),
        in_specs=[any_space] * 11,
        out_specs=vmem,
        scratch_shapes=[
            pltpu.VMEM((local_frames, n, width, channels), BF16),
            halo,
            halo,
            pltpu.VMEM((local_frames, n + 2 * HALO, width, 3 * channels), BF16),
            pltpu.VMEM((local_frames, n + 4, width, 3 * channels), BF16),
            weight,
            weight,
            pltpu.VMEM((3, channels, channels), BF16),
            square,
            square,
            square,
            square,
            weight,
            pltpu.VMEM((local_frames, 4, width, channels), F32),
            pltpu.VMEM((1, channels), F32),
            pltpu.VMEM((frame_count, frame_count), F32),
            pltpu.VMEM((2, frames_axis, local_frames, slots, channels), BF16),
            pltpu.VMEM((2, frame_count + 2, slots, channels), BF16),
            pltpu.VMEM((frame_count * GROUP, frame_count * GROUP), F32),
            square,
            square,
            pixels,
            pixels,
            pixels,
            pixels,
            pltpu.VMEM((n + 2, frame_count * cols, 3 * channels), BF16),
            pltpu.SemaphoreType.DMA((n + 16,)),
            pltpu.SemaphoreType.DMA((2,)),
            pltpu.SemaphoreType.DMA((2,)),
            pltpu.SemaphoreType.DMA((2, frames_axis)),
            pltpu.SemaphoreType.DMA((2, frames_axis)),
        ],
        compiler_params=pltpu.CompilerParams(
            collective_id=0, has_side_effects=True, vmem_limit_bytes=56 * 1024 * 1024
        ),
    )(*args)


def solution(mesh):
    placed = (P("frame", "row", None, None),) + (P(),) * 10
    return jax.shard_map(
        functools.partial(on_device, mesh.shape["frame"], mesh.shape["row"]),
        mesh=mesh,
        in_specs=placed,
        out_specs=P(None, "row", "frame", None),
        check_vma=False,
    )
```

```python
import functools
import math

import jax
import jax.numpy as jnp
from jax import lax
from jax.experimental import pallas as pl
from jax.experimental.pallas import tpu as pltpu
from jax.sharding import PartitionSpec as P

MESH = pl.DeviceIdType.MESH
BF16 = jnp.bfloat16
F32 = jnp.float32
HALO = 3
GROUP = 16


def matmul(lhs, rhs):
    return jnp.dot(lhs, rhs, preferred_element_type=F32)


def partner(index, distance, count):
    if count & (count - 1):
        return lax.rem(index + distance, count)
    bit = 1
    while bit < count:
        if distance & bit:
            index = index + bit - 2 * bit * lax.rem(lax.div(index, bit), 2)
        bit *= 2
    return index


def silu(v):
    half = 0.5 * v
    return half + half * jnp.tanh(half)


def silu_of_sum(one, two):
    half = 0.5 * one + 0.5 * two
    return half + half * jnp.tanh(half)


def steps_below(index, pitch, count):
    quotient = jnp.zeros_like(index)
    for k in range(1, count):
        quotient = quotient + (index >= k * pitch).astype(jnp.int32)
    return quotient


def shifted_columns(rows, width):
    count, _, channels = rows.shape
    flat = rows.astype(F32).reshape(count * width, channels)
    column = lax.broadcasted_iota(jnp.int32, (count, width, channels), 1)
    left = pltpu.roll(flat, 1, 0).reshape(count, width, channels)
    right = pltpu.roll(flat, count * width - 1, 0).reshape(count, width, channels)
    left = jnp.where(column == 0, 0.0, left).astype(BF16)
    right = jnp.where(column == width - 1, 0.0, right).astype(BF16)
    return left, right


def spread(dst, first_row, rows, width):
    count, _, channels = rows.shape
    left, right = shifted_columns(rows, width)
    span = slice(first_row, first_row + count)
    dst[span, :, 0:channels] = left
    dst[span, :, channels : 2 * channels] = rows
    dst[span, :, 2 * channels : 3 * channels] = right


def kernel(
    frames_axis,
    rows_axis,
    x_hbm,
    w1_hbm,
    w2_hbm,
    tk_hbm,
    gain_hbm,
    wq_hbm,
    wk_hbm,
    wv_hbm,
    wo_hbm,
    bias_hbm,
    w3_hbm,
    out_ref,
    xin,
    far_in,
    near_in,
    xs,
    fs,
    w1,
    w2,
    tk,
    wq,
    wk,
    wv,
    wo,
    w3,
    partial,
    partial3,
    gain_ref,
    bias_ref,
    packed,
    moved,
    masked_bias,
    w_score,
    w_mixed,
    cols3,
    load_sem,
    near_sem,
    halo_send,
    halo_recv,
    send_sem,
    recv_sem,
):
    frame = lax.axis_index("frame")
    row = lax.axis_index("row")
    local_frames, n, width, channels = x_hbm.shape
    frame_count = frames_axis * local_frames
    cols = width // frames_axis
    half_rows = (n + 2) // 2
    slots = packed.shape[3]

    odd = lax.rem(row, 2)
    near = row + 1 - 2 * odd
    far = lax.rem(row - 1 + 2 * odd + rows_axis, rows_axis)
    has_far = (row + odd > 0) & (row + odd < rows_axis)

    once = 1 + lax.div(frame, frames_axis)

    def stage(body):
        lax.fori_loop(0, once, lambda _, carry: (body(), carry)[1], 0)

    barrier = pltpu.get_barrier_semaphore()

    @pl.when(has_far)
    def _():
        pl.semaphore_signal(barrier, inc=1, device_id={"row": far}, device_id_type=MESH)

    @pl.when(odd == 1)
    def _():
        pl.semaphore_signal(barrier, inc=1, device_id={"row": near}, device_id_type=MESH)

    for k in range(1, frames_axis):
        peer = lax.rem(frame + k, frames_axis)
        pl.semaphore_signal(barrier, inc=1, device_id={"frame": peer}, device_id_type=MESH)

    count = [0]

    def load(src, dst):
        copy = pltpu.make_async_copy(src, dst, load_sem.at[count[0]])
        count[0] += 1
        copy.start()
        return copy

    def mirrored(i, size):
        return i + odd * (size - 1 - 2 * i)

    x_loads = [load(x_hbm.at[:, i], xin.at[:, mirrored(i, n)]) for i in range(n)]
    w1_loads = [load(w1_hbm.at[a], w1.at[mirrored(a, 3)]) for a in range(3)]
    w2_loads = [load(w2_hbm.at[a], w2.at[mirrored(a, 3)]) for a in range(3)]
    late_loads = [
        load(src, dst)
        for src, dst in (
            (tk_hbm, tk),
            (gain_hbm, gain_ref),
            (wq_hbm, wq),
            (wk_hbm, wk),
            (wv_hbm, wv),
            (bias_hbm, bias_ref),
            (wo_hbm, wo),
        )
    ]
    w3_loads = [load(w3_hbm.at[a], w3.at[mirrored(a, 3)]) for a in range(3)]

    others = has_far.astype(jnp.int32) + frames_axis - 1

    @pl.when(odd == 0)
    def _():
        pl.semaphore_wait(barrier, others + 1)
        pl.semaphore_signal(near_sem, inc=1, device_id={"row": near}, device_id_type=MESH)


    to_far = pltpu.make_async_remote_copy(
        src_ref=xin.at[:, 0:HALO],
        dst_ref=far_in,
        send_sem=halo_send.at[0],
        recv_sem=halo_recv.at[0],
        device_id={"row": far},
        device_id_type=MESH,
    )
    to_near = pltpu.make_async_remote_copy(
        src_ref=xin.at[:, n - HALO : n],
        dst_ref=near_in,
        send_sem=halo_send.at[1],
        recv_sem=halo_recv.at[1],
        device_id={"row": near},
        device_id_type=MESH,
    )
    for copy in x_loads:
        copy.wait()

    @pl.when(odd == 0)
    def _():
        pl.when(has_far)(to_far.start)
        to_near.start()

    @pl.when(odd == 1)
    def _():
        pl.semaphore_wait(near_sem, 1)
        to_near.start()
        pl.semaphore_wait(barrier, others)
        pl.when(has_far)(to_far.start)


    @pl.when(jnp.logical_not(has_far))
    def _():
        far_in[...] = jnp.zeros_like(far_in)

    inner = half_rows * cols
    edge = jnp.zeros((2, 1, slots, channels), BF16)
    moved[:, 0:1] = edge
    moved[:, frame_count + 1 : frame_count + 2] = edge

    for f in range(local_frames):
        spread(xs.at[f], HALO, xin[f], width)
    for copy in w1_loads:
        copy.wait()
    @stage
    def _():
        own_rows = xs[:, HALO : HALO + n].reshape(-1, 3 * channels)
        shares = [
            matmul(own_rows, w1[a].reshape(3 * channels, channels)).reshape(
                local_frames, n, width, channels
            )
            for a in range(3)
        ]
        partial[:, 0] = shares[2][:, 0]
        partial[:, 1] = shares[1][:, 0] + shares[2][:, 1]
        partial[:, 2] = shares[0][:, n - 2] + shares[1][:, n - 1]
        partial[:, 3] = shares[0][:, n - 1]
        for f in range(local_frames):
            whole = [
                shares[0][f, t - 1] + shares[1][f, t] + shares[2][f, t + 1] for t in range(1, n - 1)
            ]
            spread(fs.at[f], 3, silu(jnp.stack(whole)).astype(BF16), width)

    def edges(rows, a):
        part = matmul(
            rows.reshape(-1, 3 * channels), w1[a].reshape(3 * channels, channels)
        )
        return part.reshape(local_frames, -1, width, channels)

    def pack(half, second):
        none = jnp.zeros((local_frames, cols, channels), F32)
        place = lax.broadcasted_iota(jnp.int32, none.shape, 1)
        blocks = [
            [second[:, j, o * cols : (o + 1) * cols] for j in range(half_rows)]
            for o in range(frames_axis)
        ]
        for o in range(frames_axis):
            outer = none
            for side, (p, at) in enumerate(((o - 1, cols - 1), (o + 1, 0))):
                if not 0 <= p < frames_axis:
                    continue
                for j in range(half_rows):
                    to = side * half_rows + j
                    turned = pltpu.roll(blocks[p][j], (to - at) % cols, 1)
                    outer = jnp.where(place == to, turned, outer)
            packed[half, o] = jnp.concatenate([*blocks[o], outer], axis=1).astype(BF16)

    def second_half(half, first_row):
        @stage
        def _():
            def rows(a, k):
                taken = fs[:, first_row + a : first_row + a + half_rows, :, k : k + channels]
                return taken.reshape(-1, channels)

            taps = [(a, k * channels) for a in range(3) for k in range(3)]
            cut = (len(taps) + 1) // 2
            sums = []
            for some in (taps[:cut], taps[cut:]):
                total = None
                for a, k in some:
                    part = matmul(rows(a, k), w2[a].reshape(3 * channels, channels)[k : k + channels])
                    total = part if total is None else total + part
                sums.append(total)
            second = silu_of_sum(*sums).reshape(local_frames, half_rows, width, channels)
            if half == 0:
                place = lax.broadcasted_iota(jnp.int32, second.shape, 1)
                second = jnp.where((place > 0) | has_far, second, 0.0)
            pack(half, second)

        copies = []
        place = pl.ds(1 + frame * local_frames, local_frames)
        for k in reversed(range(1, frames_axis)):
            peer = partner(frame, k, frames_axis)
            copy = pltpu.make_async_remote_copy(
                src_ref=packed.at[half, peer],
                dst_ref=moved.at[half, place],
                send_sem=send_sem.at[half, k],
                recv_sem=recv_sem.at[half, k],
                device_id={"frame": peer},
                device_id_type=MESH,
            )
            copy.start()
            copies.append(copy)
        moved[half, place] = packed[half, frame]
        return copies

    to_near.wait_recv()
    for f in range(local_frames):
        spread(
            xs.at[f],
            HALO + n,
            jnp.stack([near_in[f, HALO - 1 - j] for j in range(HALO)]),
            width,
        )
    @stage
    def _():
        top = HALO + n
        two = edges(xs[:, top : top + 3], 2)
        one = edges(xs[:, top : top + 2], 1)
        zero = edges(xs[:, top : top + 1], 0)
        for f in range(local_frames):
            rows = jnp.stack(
                [
                    partial[f, 2] + two[f, 0],
                    partial[f, 3] + two[f, 1] + one[f, 0],
                    two[f, 2] + one[f, 1] + zero[f, 0],
                ]
            )
            spread(fs.at[f], n + 1, silu(rows).astype(BF16), width)

    for copy in w2_loads:
        copy.wait()
    near_copies = second_half(1, half_rows)

    pl.when(has_far)(to_far.wait_recv)
    for f in range(local_frames):
        spread(
            xs.at[f], 0, jnp.stack([far_in[f, HALO - 1 - j] for j in range(HALO)]), width
        )
    @stage
    def _():
        zero = edges(xs[:, 0:3], 0)
        one = edges(xs[:, 1:3], 1)
        two = edges(xs[:, 2:3], 2)
        for f in range(local_frames):
            rows = jnp.stack(
                [
                    zero[f, 0] + one[f, 0] + two[f, 0],
                    partial[f, 0] + zero[f, 1] + one[f, 1],
                    partial[f, 1] + zero[f, 2],
                ]
            )
            rows = silu(rows)
            place = lax.broadcasted_iota(jnp.int32, rows.shape, 0)
            rows = jnp.where((place > 1) | has_far, rows, 0.0)
            spread(fs.at[f], 0, rows.astype(BF16), width)

    far_copies = second_half(0, 0)

    for copy in late_loads:
        copy.wait()
    span = frame_count * GROUP
    lane = lax.broadcasted_iota(jnp.int32, (frame_count, span), 1)
    wide = jnp.zeros((frame_count, span), F32)
    for g in range(frame_count):
        inside = (lane >= g * GROUP) & (lane < (g + 1) * GROUP)
        wide = jnp.where(inside, bias_ref[:, g : g + 1], wide)
    wide = jnp.broadcast_to(wide[:, None, :], (frame_count, GROUP, span)).reshape(span, span)
    query_pixel = jnp.bitwise_and(lax.broadcasted_iota(jnp.int32, (span, span), 0), GROUP - 1)
    key_pixel = jnp.bitwise_and(lax.broadcasted_iota(jnp.int32, (span, span), 1), GROUP - 1)
    masked_bias[...] = jnp.where(query_pixel == key_pixel, wide, -1e30)

    @stage
    def _():
        wide = lax.dot_general(
            wq[...], wk[...], (((1,), (1,)), ((), ())), preferred_element_type=F32
        )
        w_score[...] = (wide * (1.0 / math.sqrt(channels))).astype(BF16)
        w_mixed[...] = matmul(wv[...], wo[...]).astype(BF16)

    ones = jnp.ones((span, GROUP * 8), BF16)

    def attend(half, copies, cols_row):
        for copy in copies:
            copy.wait_recv()

        @stage
        def _():
            here = moved.at[half]
            groups = [slice(g * GROUP, (g + 1) * GROUP) for g in range(slots // GROUP)]
            residual, queries, values, scores = [], [], [], []
            for part in groups:
                taps = [
                    matmul(here[tap : tap + frame_count, part].reshape(span, channels), tk[tap])
                    for tap in range(3)
                ]
                centre = here[1 : 1 + frame_count, part].reshape(span, channels).astype(F32)
                residual.append((centre + taps[0] + taps[1] + taps[2]).astype(BF16).astype(F32))
            gained = [(widened * gain_ref[...]).astype(BF16) for widened in residual]
            for r in gained:
                queries.append(matmul(r, w_score[...]).astype(BF16))
            scales = [
                lax.rsqrt(jnp.mean(widened * widened, axis=-1, keepdims=True) + 1e-06)
                for widened in residual
            ]
            keys = [
                (widened * scale * gain_ref[...]).astype(BF16)
                for widened, scale in zip(residual, scales)
            ]
            for r, scale in zip(gained, scales):
                values.append((matmul(r, w_mixed[...]) * scale).astype(BF16))
            for q, k in zip(queries, keys):
                scores.append(
                    lax.dot_general(
                        q, k, (((1,), (1,)), ((), ())), preferred_element_type=F32
                    )
                )
            scores = [
                score * scale + masked_bias[...] for score, scale in zip(scores, scales)
            ]
            peaks = [jnp.max(score, axis=-1, keepdims=True) for score in scores]
            raised = [jnp.exp(score - peak).astype(BF16) for score, peak in zip(scores, peaks)]
            parts = []
            for r, v, w in zip(raised, values, residual):
                total = matmul(r, ones)[:, 0:1]
                mixed = w + matmul(r, v) / total
                parts.append(mixed.reshape(frame_count, GROUP, channels))
            attended = jnp.concatenate(parts, axis=1)
            outer = attended[:, inner : inner + cols]
            place = lax.broadcasted_iota(jnp.int32, outer.shape, 1)
            for j in range(half_rows):
                here = attended[:, j * cols : (j + 1) * cols]
                left = jnp.where(
                    place == 0, pltpu.roll(outer, -j % cols, 1), pltpu.roll(here, 1, 1)
                )
                right = jnp.where(
                    place == cols - 1,
                    pltpu.roll(outer, (cols - 1 - half_rows - j) % cols, 1),
                    pltpu.roll(here, cols - 1, 1),
                )
                for b, part in enumerate((left, here, right)):
                    cols3[cols_row + j, :, b * channels : (b + 1) * channels] = part.reshape(
                        frame_count * cols, channels
                    ).astype(BF16)

    def third(rows, a):
        part = matmul(rows.reshape(-1, 3 * channels), w3[a].reshape(3 * channels, channels))
        return part.reshape(-1, frame_count, cols, channels)

    attend(1, near_copies, half_rows)
    for copy in w3_loads:
        copy.wait()

    @stage
    def _():
        two = third(cols3[half_rows : n + 2], 2)
        one = third(cols3[half_rows : n + 1], 1)
        zero = third(cols3[half_rows:n], 0)
        partial3[0] = two[0]
        partial3[1] = two[1] + one[0]
        out_ref[:, mirrored(n - 1, n)] = (two[2] + one[1] + zero[0]).astype(BF16)

    attend(0, far_copies, 0)

    @stage
    def _():
        zero = third(cols3[0:half_rows], 0)
        one = third(cols3[1:half_rows], 1)
        two = third(cols3[2:half_rows], 2)
        out_ref[:, mirrored(0, n)] = (zero[0] + one[0] + two[0]).astype(BF16)
        out_ref[:, mirrored(1, n)] = (partial3[0] + zero[1] + one[1]).astype(BF16)
        out_ref[:, mirrored(2, n)] = (partial3[1] + zero[2]).astype(BF16)

    pl.when(has_far)(to_far.wait_send)
    to_near.wait_send()
    for copy in near_copies + far_copies:
        copy.wait_send()


def on_device(frames_axis, rows_axis, *args):
    frames_in = args[0]
    norm_gain = args[4]
    local_frames, n, width, channels = frames_in.shape
    frame_count = local_frames * frames_axis
    cols = width // frames_axis
    half_rows = (n + 2) // 2
    slots = -(-half_rows * (cols + 2) // GROUP) * GROUP
    args = args[:4] + (norm_gain.reshape(1, channels),) + args[5:]
    any_space = pl.BlockSpec(memory_space=pl.ANY)
    vmem = pl.BlockSpec(memory_space=pltpu.VMEM)
    weight = pltpu.VMEM((3, 3, channels, channels), BF16)
    square = pltpu.VMEM((channels, channels), BF16)
    halo = pltpu.VMEM((local_frames, HALO, width, channels), BF16)
    return pl.pallas_call(
        functools.partial(kernel, frames_axis, rows_axis),
        out_shape=pltpu.VMEM((frame_count, n, cols, channels), BF16),
        in_specs=[any_space] * 11,
        out_specs=vmem,
        scratch_shapes=[
            pltpu.VMEM((local_frames, n, width, channels), BF16),
            halo,
            halo,
            pltpu.VMEM((local_frames, n + 2 * HALO, width, 3 * channels), BF16),
            pltpu.VMEM((local_frames, n + 4, width, 3 * channels), BF16),
            weight,
            weight,
            pltpu.VMEM((3, channels, channels), BF16),
            square,
            square,
            square,
            square,
            weight,
            pltpu.VMEM((local_frames, 4, width, channels), F32),
            pltpu.VMEM((2, frame_count, cols, channels), F32),
            pltpu.VMEM((1, channels), F32),
            pltpu.VMEM((frame_count, frame_count), F32),
            pltpu.VMEM((2, frames_axis, local_frames, slots, channels), BF16),
            pltpu.VMEM((2, frame_count + 2, slots, channels), BF16),
            pltpu.VMEM((frame_count * GROUP, frame_count * GROUP), F32),
            square,
            square,
            pltpu.VMEM((n + 2, frame_count * cols, 3 * channels), BF16),
            pltpu.SemaphoreType.DMA((n + 16,)),
            pltpu.SemaphoreType.REGULAR,
            pltpu.SemaphoreType.DMA((2,)),
            pltpu.SemaphoreType.DMA((2,)),
            pltpu.SemaphoreType.DMA((2, frames_axis)),
            pltpu.SemaphoreType.DMA((2, frames_axis)),
        ],
        compiler_params=pltpu.CompilerParams(
            collective_id=0, has_side_effects=True, vmem_limit_bytes=56 * 1024 * 1024
        ),
    )(*args)


def solution(mesh):
    placed = (P("frame", "row", None, None),) + (P(),) * 10
    return jax.shard_map(
        functools.partial(on_device, mesh.shape["frame"], mesh.shape["row"]),
        mesh=mesh,
        in_specs=placed,
        out_specs=P(None, "row", "frame", None),
        check_vma=False,
    )
```

```python
import functools
import math

import jax
import jax.numpy as jnp
from jax import lax
from jax.experimental import pallas as pl
from jax.experimental.pallas import tpu as pltpu
from jax.sharding import PartitionSpec as P

MESH = pl.DeviceIdType.MESH
BF16 = jnp.bfloat16
F32 = jnp.float32
HALO = 3
GROUP = 16


def matmul(lhs, rhs):
    return jnp.dot(lhs, rhs, preferred_element_type=F32)


def partner(index, distance, count):
    if count & (count - 1):
        return lax.rem(index + distance, count)
    bit = 1
    while bit < count:
        if distance & bit:
            index = index + bit - 2 * bit * lax.rem(lax.div(index, bit), 2)
        bit *= 2
    return index


def silu(v):
    half = 0.5 * v
    return half + half * jnp.tanh(half)


def silu_of_sum(one, two):
    half = 0.5 * one + 0.5 * two
    return half + half * jnp.tanh(half)


def steps_below(index, pitch, count):
    quotient = jnp.zeros_like(index)
    for k in range(1, count):
        quotient = quotient + (index >= k * pitch).astype(jnp.int32)
    return quotient


def shifted_columns(rows, width):
    count, _, channels = rows.shape
    flat = rows.astype(F32).reshape(count * width, channels)
    column = lax.broadcasted_iota(jnp.int32, (count, width, channels), 1)
    left = pltpu.roll(flat, 1, 0).reshape(count, width, channels)
    right = pltpu.roll(flat, count * width - 1, 0).reshape(count, width, channels)
    left = jnp.where(column == 0, 0.0, left).astype(BF16)
    right = jnp.where(column == width - 1, 0.0, right).astype(BF16)
    return left, right


def spread(dst, first_row, rows, width):
    count, _, channels = rows.shape
    left, right = shifted_columns(rows, width)
    span = slice(first_row, first_row + count)
    dst[span, :, 0:channels] = left
    dst[span, :, channels : 2 * channels] = rows
    dst[span, :, 2 * channels : 3 * channels] = right


def kernel(
    frames_axis,
    rows_axis,
    x_hbm,
    w1_hbm,
    w2_hbm,
    tk_hbm,
    gain_hbm,
    wq_hbm,
    wk_hbm,
    wv_hbm,
    wo_hbm,
    bias_hbm,
    w3_hbm,
    out_ref,
    xin,
    far_in,
    near_in,
    xs,
    fs,
    w1,
    w2,
    tk,
    wq,
    wk,
    wv,
    wo,
    w3,
    partial,
    partial3,
    gain_ref,
    bias_ref,
    packed,
    moved,
    masked_bias,
    w_score,
    w_mixed,
    cols3,
    load_sem,
    near_sem,
    peer_sem,
    go_sem,
    halo_send,
    halo_recv,
    send_sem,
    recv_sem,
):
    frame = lax.axis_index("frame")
    row = lax.axis_index("row")
    local_frames, n, width, channels = x_hbm.shape
    frame_count = frames_axis * local_frames
    cols = width // frames_axis
    half_rows = (n + 2) // 2
    slots = packed.shape[3]

    odd = lax.rem(row, 2)
    near = row + 1 - 2 * odd
    far = lax.rem(row - 1 + 2 * odd + rows_axis, rows_axis)
    has_far = (row + odd > 0) & (row + odd < rows_axis)

    once = 1 + lax.div(frame, frames_axis)

    def stage(body, wanted=None):
        steps = once if wanted is None else once * wanted
        lax.fori_loop(0, steps, lambda _, carry: (body(), carry)[1], 0)

    barrier = pltpu.get_barrier_semaphore()
    peers = [lax.rem(frame + k, frames_axis) for k in range(1, frames_axis)]
    others = has_far.astype(jnp.int32)

    def signal(semaphore, **place):
        pl.semaphore_signal(semaphore, inc=1, device_id=place, device_id_type=MESH)

    @pl.when(has_far)
    def _():
        signal(barrier, row=far)

    @pl.when(odd == 1)
    def _():
        signal(barrier, row=near)
        for peer in peers:
            signal(barrier, frame=peer)

    def halo(side, source):
        far_side = side == 0
        from_top = odd if far_side else 1 - odd
        return pltpu.make_async_remote_copy(
            src_ref=source.at[:, pl.ds(from_top * (n - HALO), HALO)],
            dst_ref=far_in if far_side else near_in,
            send_sem=halo_send.at[side],
            recv_sem=halo_recv.at[side],
            device_id={"row": far if far_side else near},
            device_id_type=MESH,
        )

    to_far, to_near = halo(0, xin), halo(1, xin)

    @pl.when(odd == 0)
    def _():
        pl.semaphore_wait(barrier, others + 1)
        signal(near_sem, row=near)
        pl.when(has_far)(halo(0, x_hbm).start)

    count = [0]

    def load(src, dst):
        copy = pltpu.make_async_copy(src, dst, load_sem.at[count[0]])
        count[0] += 1
        copy.start()
        return copy

    def mirrored(i, size):
        return i + odd * (size - 1 - 2 * i)

    x_loads = [load(x_hbm, xin)]
    w1_loads = [load(w1_hbm, w1)]
    w2_loads = [load(w2_hbm, w2)]
    late_loads = [
        load(src, dst)
        for src, dst in (
            (tk_hbm, tk),
            (gain_hbm, gain_ref),
            (wq_hbm, wq),
            (wk_hbm, wk),
            (wv_hbm, wv),
            (bias_hbm, bias_ref),
            (wo_hbm, wo),
        )
    ]
    w3_loads = [load(w3_hbm, w3)]
    for copy in x_loads:
        copy.wait()
    pl.when(odd == 0)(to_near.start)

    @pl.when(odd == 1)
    def _():
        pl.semaphore_wait(near_sem, 1)
        to_near.start()
        pl.semaphore_wait(barrier, others + frames_axis - 1)
        pl.when(has_far)(to_far.start)
        for peer in peers:
            signal(peer_sem, frame=peer)

    @pl.when(jnp.logical_not(has_far))
    def _():
        far_in[...] = jnp.zeros_like(far_in)

    inner = half_rows * cols
    edge = jnp.zeros((2, 1, slots, channels), BF16)
    moved[:, 0:1] = edge
    moved[:, frame_count + 1 : frame_count + 2] = edge

    for f in range(local_frames):
        spread(xs.at[f], HALO, jnp.stack([xin[f, mirrored(t, n)] for t in range(n)]), width)
    for copy in w1_loads:
        copy.wait()
    @stage
    def _():
        own_rows = xs[:, HALO : HALO + n].reshape(-1, 3 * channels)
        shares = [
            matmul(own_rows, w1[mirrored(a, 3)].reshape(3 * channels, channels)).reshape(
                local_frames, n, width, channels
            )
            for a in range(3)
        ]
        partial[:, 0] = shares[2][:, 0]
        partial[:, 1] = shares[1][:, 0] + shares[2][:, 1]
        partial[:, 2] = shares[0][:, n - 2] + shares[1][:, n - 1]
        partial[:, 3] = shares[0][:, n - 1]
        for f in range(local_frames):
            whole = [
                shares[0][f, t - 1] + shares[1][f, t] + shares[2][f, t + 1] for t in range(1, n - 1)
            ]
            spread(fs.at[f], 3, silu(jnp.stack(whole)).astype(BF16), width)

    def edges(rows, a):
        part = matmul(
            rows.reshape(-1, 3 * channels), w1[mirrored(a, 3)].reshape(3 * channels, channels)
        )
        return part.reshape(local_frames, -1, width, channels)

    def pack(half, second):
        none = jnp.zeros((local_frames, cols, channels), F32)
        place = lax.broadcasted_iota(jnp.int32, none.shape, 1)
        blocks = [
            [second[:, j, o * cols : (o + 1) * cols] for j in range(half_rows)]
            for o in range(frames_axis)
        ]
        for o in range(frames_axis):
            outer = none
            for side, (p, at) in enumerate(((o - 1, cols - 1), (o + 1, 0))):
                if not 0 <= p < frames_axis:
                    continue
                for j in range(half_rows):
                    to = side * half_rows + j
                    turned = pltpu.roll(blocks[p][j], (to - at) % cols, 1)
                    outer = jnp.where(place == to, turned, outer)
            packed[half, o] = jnp.concatenate([*blocks[o], outer], axis=1).astype(BF16)

    def second_half(half, first_row):
        @stage
        def _():
            def rows(a, k):
                taken = fs[:, first_row + a : first_row + a + half_rows, :, k : k + channels]
                return taken.reshape(-1, channels)

            taps = [(a, k * channels) for a in range(3) for k in range(3)]
            cut = (len(taps) + 1) // 2
            sums = []
            for some in (taps[:cut], taps[cut:]):
                total = None
                for a, k in some:
                    part = matmul(rows(a, k), w2[mirrored(a, 3)].reshape(3 * channels, channels)[k : k + channels])
                    total = part if total is None else total + part
                sums.append(total)
            second = silu_of_sum(*sums).reshape(local_frames, half_rows, width, channels)
            if half == 0:
                place = lax.broadcasted_iota(jnp.int32, second.shape, 1)
                second = jnp.where((place > 0) | has_far, second, 0.0)
            pack(half, second)

        copies = []
        if half == 1:

            @pl.when(odd == 0)
            def _():
                pl.semaphore_wait(go_sem, 1)

        place = pl.ds(1 + frame * local_frames, local_frames)
        for k in reversed(range(1, frames_axis)):
            peer = partner(frame, k, frames_axis)
            copy = pltpu.make_async_remote_copy(
                src_ref=packed.at[half, peer],
                dst_ref=moved.at[half, place],
                send_sem=send_sem.at[half, k],
                recv_sem=recv_sem.at[half, k],
                device_id={"frame": peer},
                device_id_type=MESH,
            )
            copy.start()
            copies.append(copy)
        moved[half, place] = packed[half, frame]
        return copies

    to_near.wait_recv()
    for f in range(local_frames):
        spread(
            xs.at[f],
            HALO + n,
            jnp.stack([near_in[f, j + odd * (HALO - 1 - 2 * j)] for j in range(HALO)]),
            width,
        )
    @stage
    def _():
        top = HALO + n
        two = edges(xs[:, top : top + 3], 2)
        one = edges(xs[:, top : top + 2], 1)
        zero = edges(xs[:, top : top + 1], 0)
        for f in range(local_frames):
            rows = jnp.stack(
                [
                    partial[f, 2] + two[f, 0],
                    partial[f, 3] + two[f, 1] + one[f, 0],
                    two[f, 2] + one[f, 1] + zero[f, 0],
                ]
            )
            spread(fs.at[f], n + 1, silu(rows).astype(BF16), width)

    for copy in w2_loads:
        copy.wait()

    @pl.when(odd == 1)
    def _():
        pl.semaphore_wait(peer_sem, frames_axis - 1)
        signal(go_sem, row=near)

    near_copies = second_half(1, half_rows)

    pl.when(has_far)(to_far.wait_recv)
    for f in range(local_frames):
        spread(
            xs.at[f], 0, jnp.stack([far_in[f, j + odd * (HALO - 1 - 2 * j)] for j in range(HALO)]), width
        )
    @stage
    def _():
        zero = edges(xs[:, 0:3], 0)
        one = edges(xs[:, 1:3], 1)
        two = edges(xs[:, 2:3], 2)
        for f in range(local_frames):
            rows = jnp.stack(
                [
                    zero[f, 0] + one[f, 0] + two[f, 0],
                    partial[f, 0] + zero[f, 1] + one[f, 1],
                    partial[f, 1] + zero[f, 2],
                ]
            )
            rows = silu(rows)
            place = lax.broadcasted_iota(jnp.int32, rows.shape, 0)
            rows = jnp.where((place > 1) | has_far, rows, 0.0)
            spread(fs.at[f], 0, rows.astype(BF16), width)

    far_copies = second_half(0, 0)

    for copy in late_loads:
        copy.wait()
    span = frame_count * GROUP
    lane = lax.broadcasted_iota(jnp.int32, (frame_count, span), 1)
    wide = jnp.zeros((frame_count, span), F32)
    for g in range(frame_count):
        inside = (lane >= g * GROUP) & (lane < (g + 1) * GROUP)
        wide = jnp.where(inside, bias_ref[:, g : g + 1], wide)
    wide = jnp.broadcast_to(wide[:, None, :], (frame_count, GROUP, span)).reshape(span, span)
    query_pixel = jnp.bitwise_and(lax.broadcasted_iota(jnp.int32, (span, span), 0), GROUP - 1)
    key_pixel = jnp.bitwise_and(lax.broadcasted_iota(jnp.int32, (span, span), 1), GROUP - 1)
    masked_bias[...] = jnp.where(query_pixel == key_pixel, wide, -1e30)

    @stage
    def _():
        wide = lax.dot_general(
            wq[...], wk[...], (((1,), (1,)), ((), ())), preferred_element_type=F32
        )
        w_score[...] = (wide * (1.0 / math.sqrt(channels))).astype(BF16)
        w_mixed[...] = matmul(wv[...], wo[...]).astype(BF16)

    ones = jnp.ones((span, GROUP * 8), BF16)

    def attend(half, copies, cols_row):
        for copy in copies:
            copy.wait_recv()

        @stage
        def _():
            here = moved.at[half]
            groups = [slice(g * GROUP, (g + 1) * GROUP) for g in range(slots // GROUP)]
            residual, queries, values, scores = [], [], [], []
            for part in groups:
                taps = [
                    matmul(here[tap : tap + frame_count, part].reshape(span, channels), tk[tap])
                    for tap in range(3)
                ]
                centre = here[1 : 1 + frame_count, part].reshape(span, channels).astype(F32)
                residual.append((centre + taps[0] + taps[1] + taps[2]).astype(BF16).astype(F32))
            gained = [(widened * gain_ref[...]).astype(BF16) for widened in residual]
            for r in gained:
                queries.append(matmul(r, w_score[...]).astype(BF16))
            scales = [
                lax.rsqrt(jnp.mean(widened * widened, axis=-1, keepdims=True) + 1e-06)
                for widened in residual
            ]
            keys = [
                (widened * scale * gain_ref[...]).astype(BF16)
                for widened, scale in zip(residual, scales)
            ]
            for r, scale in zip(gained, scales):
                values.append((matmul(r, w_mixed[...]) * scale).astype(BF16))
            for q, k in zip(queries, keys):
                scores.append(
                    lax.dot_general(
                        q, k, (((1,), (1,)), ((), ())), preferred_element_type=F32
                    )
                )
            scores = [
                score * scale + masked_bias[...] for score, scale in zip(scores, scales)
            ]
            peaks = [jnp.max(score, axis=-1, keepdims=True) for score in scores]
            raised = [jnp.exp(score - peak).astype(BF16) for score, peak in zip(scores, peaks)]
            parts = []
            for r, v, w in zip(raised, values, residual):
                total = matmul(r, ones)[:, 0:1]
                mixed = w + matmul(r, v) / total
                parts.append(mixed.reshape(frame_count, GROUP, channels))
            attended = jnp.concatenate(parts, axis=1)
            outer = attended[:, inner : inner + cols]
            place = lax.broadcasted_iota(jnp.int32, outer.shape, 1)
            for j in range(half_rows):
                here = attended[:, j * cols : (j + 1) * cols]
                left = jnp.where(
                    place == 0, pltpu.roll(outer, -j % cols, 1), pltpu.roll(here, 1, 1)
                )
                right = jnp.where(
                    place == cols - 1,
                    pltpu.roll(outer, (cols - 1 - half_rows - j) % cols, 1),
                    pltpu.roll(here, cols - 1, 1),
                )
                for b, part in enumerate((left, here, right)):
                    cols3[cols_row + j, :, b * channels : (b + 1) * channels] = part.reshape(
                        frame_count * cols, channels
                    ).astype(BF16)

    def third(rows, a):
        part = matmul(rows.reshape(-1, 3 * channels), w3[mirrored(a, 3)].reshape(3 * channels, channels))
        return part.reshape(-1, frame_count, cols, channels)

    attend(1, near_copies, half_rows)
    for copy in w3_loads:
        copy.wait()

    def near_third():
        two = third(cols3[half_rows : n + 2], 2)
        one = third(cols3[half_rows : n + 1], 1)
        zero = third(cols3[half_rows:n], 0)
        partial3[0] = two[0]
        partial3[1] = two[1] + one[0]
        out_ref[:, mirrored(n - 1, n)] = (two[2] + one[1] + zero[0]).astype(BF16)

    def far_third():
        zero = third(cols3[0:half_rows], 0)
        one = third(cols3[1:half_rows], 1)
        two = third(cols3[2:half_rows], 2)
        out_ref[:, mirrored(0, n)] = (zero[0] + one[0] + two[0]).astype(BF16)
        out_ref[:, mirrored(1, n)] = (partial3[0] + zero[1] + one[1]).astype(BF16)
        out_ref[:, mirrored(2, n)] = (partial3[1] + zero[2]).astype(BF16)

    def whole_third():
        sums = [third(cols3[a : a + n], a) for a in range(3)]
        summed = sums[0] + sums[1] + sums[2]
        for t in range(n):
            out_ref[:, mirrored(t, n)] = summed[t].astype(BF16)

    stage(near_third, others)
    attend(0, far_copies, 0)
    stage(far_third, others)
    stage(whole_third, 1 - others)

    pl.when(has_far)(to_far.wait_send)
    to_near.wait_send()
    for copy in near_copies + far_copies:
        copy.wait_send()


def on_device(frames_axis, rows_axis, *args):
    frames_in = args[0]
    norm_gain = args[4]
    local_frames, n, width, channels = frames_in.shape
    frame_count = local_frames * frames_axis
    cols = width // frames_axis
    half_rows = (n + 2) // 2
    slots = -(-half_rows * (cols + 2) // GROUP) * GROUP
    args = args[:4] + (norm_gain.reshape(1, channels),) + args[5:]
    any_space = pl.BlockSpec(memory_space=pl.ANY)
    vmem = pl.BlockSpec(memory_space=pltpu.VMEM)
    weight = pltpu.VMEM((3, 3, channels, channels), BF16)
    square = pltpu.VMEM((channels, channels), BF16)
    halo = pltpu.VMEM((local_frames, HALO, width, channels), BF16)
    return pl.pallas_call(
        functools.partial(kernel, frames_axis, rows_axis),
        out_shape=pltpu.VMEM((frame_count, n, cols, channels), BF16),
        in_specs=[any_space] * 11,
        out_specs=vmem,
        scratch_shapes=[
            pltpu.VMEM((local_frames, n, width, channels), BF16),
            halo,
            halo,
            pltpu.VMEM((local_frames, n + 2 * HALO, width, 3 * channels), BF16),
            pltpu.VMEM((local_frames, n + 4, width, 3 * channels), BF16),
            weight,
            weight,
            pltpu.VMEM((3, channels, channels), BF16),
            square,
            square,
            square,
            square,
            weight,
            pltpu.VMEM((local_frames, 4, width, channels), F32),
            pltpu.VMEM((2, frame_count, cols, channels), F32),
            pltpu.VMEM((1, channels), F32),
            pltpu.VMEM((frame_count, frame_count), F32),
            pltpu.VMEM((2, frames_axis, local_frames, slots, channels), BF16),
            pltpu.VMEM((2, frame_count + 2, slots, channels), BF16),
            pltpu.VMEM((frame_count * GROUP, frame_count * GROUP), F32),
            square,
            square,
            pltpu.VMEM((n + 2, frame_count * cols, 3 * channels), BF16),
            pltpu.SemaphoreType.DMA((11,)),
            pltpu.SemaphoreType.REGULAR,
            pltpu.SemaphoreType.REGULAR,
            pltpu.SemaphoreType.REGULAR,
            pltpu.SemaphoreType.DMA((2,)),
            pltpu.SemaphoreType.DMA((2,)),
            pltpu.SemaphoreType.DMA((2, frames_axis)),
            pltpu.SemaphoreType.DMA((2, frames_axis)),
        ],
        compiler_params=pltpu.CompilerParams(
            collective_id=0, has_side_effects=True, vmem_limit_bytes=56 * 1024 * 1024
        ),
    )(*args)


def solution(mesh):
    placed = (P("frame", "row", None, None),) + (P(),) * 10
    return jax.shard_map(
        functools.partial(on_device, mesh.shape["frame"], mesh.shape["row"]),
        mesh=mesh,
        in_specs=placed,
        out_specs=P(None, "row", "frame", None),
        check_vma=False,
    )
```

```python
import functools
import math

import jax
import jax.numpy as jnp
from jax import lax
from jax.experimental import pallas as pl
from jax.experimental.pallas import tpu as pltpu
from jax.sharding import PartitionSpec as P

MESH = pl.DeviceIdType.MESH
BF16 = jnp.bfloat16
F32 = jnp.float32
HALO = 3
GROUP = 16


def matmul(lhs, rhs):
    return jnp.dot(lhs, rhs, preferred_element_type=F32)


def partner(index, distance, count):
    if count & (count - 1):
        return lax.rem(index + distance, count)
    bit = 1
    while bit < count:
        if distance & bit:
            index = index + bit - 2 * bit * lax.rem(lax.div(index, bit), 2)
        bit *= 2
    return index


def silu(v):
    half = 0.5 * v
    return half + half * jnp.tanh(half)


def silu_of_sum(one, two):
    half = 0.5 * one + 0.5 * two
    return half + half * jnp.tanh(half)


def steps_below(index, pitch, count):
    quotient = jnp.zeros_like(index)
    for k in range(1, count):
        quotient = quotient + (index >= k * pitch).astype(jnp.int32)
    return quotient


def shifted_columns(rows, width):
    count, _, channels = rows.shape
    flat = rows.astype(F32).reshape(count * width, channels)
    column = lax.broadcasted_iota(jnp.int32, (count, width, channels), 1)
    left = pltpu.roll(flat, 1, 0).reshape(count, width, channels)
    right = pltpu.roll(flat, count * width - 1, 0).reshape(count, width, channels)
    left = jnp.where(column == 0, 0.0, left).astype(BF16)
    right = jnp.where(column == width - 1, 0.0, right).astype(BF16)
    return left, right


def spread(dst, first_row, rows, width):
    count, _, channels = rows.shape
    left, right = shifted_columns(rows, width)
    span = slice(first_row, first_row + count)
    dst[span, :, 0:channels] = left
    dst[span, :, channels : 2 * channels] = rows
    dst[span, :, 2 * channels : 3 * channels] = right


def kernel(
    frames_axis,
    rows_axis,
    x_hbm,
    w1_hbm,
    w2_hbm,
    tk_hbm,
    gain_hbm,
    wq_hbm,
    wk_hbm,
    wv_hbm,
    wo_hbm,
    bias_hbm,
    w3_hbm,
    out_ref,
    xin,
    far_in,
    near_in,
    xs,
    fs,
    w1,
    w2,
    tk,
    wq,
    wk,
    wv,
    wo,
    w3,
    partial,
    partial3,
    gain_ref,
    bias_ref,
    packed,
    moved,
    masked_bias,
    w_score,
    w_mixed,
    cols3,
    load_sem,
    near_sem,
    peer_sem,
    go_sem,
    halo_send,
    halo_recv,
    send_sem,
    recv_sem,
):
    frame = lax.axis_index("frame")
    row = lax.axis_index("row")
    local_frames, n, width, channels = x_hbm.shape
    frame_count = frames_axis * local_frames
    cols = width // frames_axis
    half_rows = (n + 2) // 2
    slots = packed.shape[3]

    odd = lax.rem(row, 2)
    near = row + 1 - 2 * odd
    far = lax.rem(row - 1 + 2 * odd + rows_axis, rows_axis)
    has_far = (row + odd > 0) & (row + odd < rows_axis)

    once = 1 + lax.div(frame, frames_axis)

    def stage(body, wanted=None):
        steps = once if wanted is None else once * wanted
        lax.fori_loop(0, steps, lambda _, carry: (body(), carry)[1], 0)

    barrier = pltpu.get_barrier_semaphore()
    peers = [lax.rem(frame + k, frames_axis) for k in range(1, frames_axis)]
    others = has_far.astype(jnp.int32)

    def signal(semaphore, **place):
        pl.semaphore_signal(semaphore, inc=1, device_id=place, device_id_type=MESH)

    @pl.when(has_far)
    def _():
        signal(barrier, row=far)

    @pl.when(odd == 1)
    def _():
        signal(barrier, row=near)
        for peer in peers:
            signal(barrier, frame=peer)

    def halo(side, source):
        far_side = side == 0
        from_top = odd if far_side else 1 - odd
        return pltpu.make_async_remote_copy(
            src_ref=source.at[:, pl.ds(from_top * (n - HALO), HALO)],
            dst_ref=far_in if far_side else near_in,
            send_sem=halo_send.at[side],
            recv_sem=halo_recv.at[side],
            device_id={"row": far if far_side else near},
            device_id_type=MESH,
        )

    to_far, to_near = halo(0, xin), halo(1, xin)

    count = [0]

    def load(src, dst):
        copy = pltpu.make_async_copy(src, dst, load_sem.at[count[0]])
        count[0] += 1
        return copy

    def mirrored(i, size):
        return i + odd * (size - 1 - 2 * i)

    x_loads = [load(x_hbm, xin)]
    w1_loads = [load(w1_hbm, w1)]
    w2_loads = [load(w2_hbm, w2)]
    late_loads = [
        load(src, dst)
        for src, dst in (
            (tk_hbm, tk),
            (gain_hbm, gain_ref),
            (wq_hbm, wq),
            (wk_hbm, wk),
            (wv_hbm, wv),
            (bias_hbm, bias_ref),
            (wo_hbm, wo),
        )
    ]
    w3_loads = [load(w3_hbm, w3)]
    for copy in x_loads:
        copy.start()
    all_loads = w1_loads + w2_loads + late_loads + w3_loads

    def start_loads():
        for copy in all_loads:
            copy.start()

    halo_first = has_far & (odd == 0)
    pl.when(jnp.logical_not(halo_first))(start_loads)

    @pl.when(odd == 0)
    def _():
        pl.semaphore_wait(barrier, others + 1)
        signal(near_sem, row=near)
        pl.when(has_far)(halo(0, x_hbm).start)

    pl.when(halo_first)(start_loads)
    for copy in x_loads:
        copy.wait()
    pl.when(odd == 0)(to_near.start)

    @pl.when(odd == 1)
    def _():
        pl.semaphore_wait(near_sem, 1)
        to_near.start()
        pl.semaphore_wait(barrier, others + frames_axis - 1)
        pl.when(has_far)(to_far.start)
        for peer in peers:
            signal(peer_sem, frame=peer)

    @pl.when(jnp.logical_not(has_far))
    def _():
        far_in[...] = jnp.zeros_like(far_in)

    inner = half_rows * cols
    edge = jnp.zeros((2, 1, slots, channels), BF16)
    moved[:, 0:1] = edge
    moved[:, frame_count + 1 : frame_count + 2] = edge

    for f in range(local_frames):
        spread(xs.at[f], HALO, jnp.stack([xin[f, mirrored(t, n)] for t in range(n)]), width)
    for copy in w1_loads:
        copy.wait()
    @stage
    def _():
        own_rows = xs[:, HALO : HALO + n].reshape(-1, 3 * channels)
        shares = [
            matmul(own_rows, w1[mirrored(a, 3)].reshape(3 * channels, channels)).reshape(
                local_frames, n, width, channels
            )
            for a in range(3)
        ]
        partial[:, 0] = shares[2][:, 0]
        partial[:, 1] = shares[1][:, 0] + shares[2][:, 1]
        partial[:, 2] = shares[0][:, n - 2] + shares[1][:, n - 1]
        partial[:, 3] = shares[0][:, n - 1]
        for f in range(local_frames):
            whole = [
                shares[0][f, t - 1] + shares[1][f, t] + shares[2][f, t + 1] for t in range(1, n - 1)
            ]
            spread(fs.at[f], 3, silu(jnp.stack(whole)).astype(BF16), width)

    def edges(rows, a):
        part = matmul(
            rows.reshape(-1, 3 * channels), w1[mirrored(a, 3)].reshape(3 * channels, channels)
        )
        return part.reshape(local_frames, -1, width, channels)

    def pack(half, second):
        none = jnp.zeros((local_frames, cols, channels), F32)
        place = lax.broadcasted_iota(jnp.int32, none.shape, 1)
        blocks = [
            [second[:, j, o * cols : (o + 1) * cols] for j in range(half_rows)]
            for o in range(frames_axis)
        ]
        for o in range(frames_axis):
            outer = none
            for side, (p, at) in enumerate(((o - 1, cols - 1), (o + 1, 0))):
                if not 0 <= p < frames_axis:
                    continue
                for j in range(half_rows):
                    to = 2 * j + side
                    turned = pltpu.roll(blocks[p][j], (to - at) % cols, 1)
                    outer = jnp.where(place == to, turned, outer)
            packed[half, o] = jnp.concatenate([*blocks[o], outer], axis=1).astype(BF16)

    def second_half(half, first_row):
        @stage
        def _():
            def rows(a, k):
                taken = fs[:, first_row + a : first_row + a + half_rows, :, k : k + channels]
                return taken.reshape(-1, channels)

            taps = [(a, k * channels) for a in range(3) for k in range(3)]
            cut = (len(taps) + 1) // 2
            sums = []
            for some in (taps[:cut], taps[cut:]):
                total = None
                for a, k in some:
                    part = matmul(rows(a, k), w2[mirrored(a, 3)].reshape(3 * channels, channels)[k : k + channels])
                    total = part if total is None else total + part
                sums.append(total)
            second = silu_of_sum(*sums).reshape(local_frames, half_rows, width, channels)
            if half == 0:
                place = lax.broadcasted_iota(jnp.int32, second.shape, 1)
                second = jnp.where((place > 0) | has_far, second, 0.0)
            pack(half, second)

        copies = []
        if half == 1:

            @pl.when(odd == 0)
            def _():
                pl.semaphore_wait(go_sem, 1)

        place = pl.ds(1 + frame * local_frames, local_frames)
        for k in reversed(range(1, frames_axis)):
            peer = partner(frame, k, frames_axis)
            copy = pltpu.make_async_remote_copy(
                src_ref=packed.at[half, peer],
                dst_ref=moved.at[half, place],
                send_sem=send_sem.at[half, k],
                recv_sem=recv_sem.at[half, k],
                device_id={"frame": peer},
                device_id_type=MESH,
            )
            copy.start()
            copies.append(copy)
        moved[half, place] = packed[half, frame]
        return copies

    to_near.wait_recv()
    for f in range(local_frames):
        spread(
            xs.at[f],
            HALO + n,
            jnp.stack([near_in[f, j + odd * (HALO - 1 - 2 * j)] for j in range(HALO)]),
            width,
        )
    @stage
    def _():
        top = HALO + n
        two = edges(xs[:, top : top + 3], 2)
        one = edges(xs[:, top : top + 2], 1)
        zero = edges(xs[:, top : top + 1], 0)
        for f in range(local_frames):
            rows = jnp.stack(
                [
                    partial[f, 2] + two[f, 0],
                    partial[f, 3] + two[f, 1] + one[f, 0],
                    two[f, 2] + one[f, 1] + zero[f, 0],
                ]
            )
            spread(fs.at[f], n + 1, silu(rows).astype(BF16), width)

    for copy in w2_loads:
        copy.wait()

    @pl.when(odd == 1)
    def _():
        pl.semaphore_wait(peer_sem, frames_axis - 1)
        signal(go_sem, row=near)

    near_copies = second_half(1, half_rows)

    pl.when(has_far)(to_far.wait_recv)
    for f in range(local_frames):
        spread(
            xs.at[f], 0, jnp.stack([far_in[f, j + odd * (HALO - 1 - 2 * j)] for j in range(HALO)]), width
        )
    @stage
    def _():
        zero = edges(xs[:, 0:3], 0)
        one = edges(xs[:, 1:3], 1)
        two = edges(xs[:, 2:3], 2)
        for f in range(local_frames):
            rows = jnp.stack(
                [
                    zero[f, 0] + one[f, 0] + two[f, 0],
                    partial[f, 0] + zero[f, 1] + one[f, 1],
                    partial[f, 1] + zero[f, 2],
                ]
            )
            rows = silu(rows)
            place = lax.broadcasted_iota(jnp.int32, rows.shape, 0)
            rows = jnp.where((place > 1) | has_far, rows, 0.0)
            spread(fs.at[f], 0, rows.astype(BF16), width)

    far_copies = second_half(0, 0)

    for copy in late_loads:
        copy.wait()
    span = frame_count * GROUP
    lane = lax.broadcasted_iota(jnp.int32, (frame_count, span), 1)
    wide = jnp.zeros((frame_count, span), F32)
    for g in range(frame_count):
        inside = (lane >= g * GROUP) & (lane < (g + 1) * GROUP)
        wide = jnp.where(inside, bias_ref[:, g : g + 1], wide)
    wide = jnp.broadcast_to(wide[:, None, :], (frame_count, GROUP, span)).reshape(span, span)
    query_pixel = jnp.bitwise_and(lax.broadcasted_iota(jnp.int32, (span, span), 0), GROUP - 1)
    key_pixel = jnp.bitwise_and(lax.broadcasted_iota(jnp.int32, (span, span), 1), GROUP - 1)
    masked_bias[...] = jnp.where(query_pixel == key_pixel, wide, -1e30)

    @stage
    def _():
        wide = lax.dot_general(
            wq[...], wk[...], (((1,), (1,)), ((), ())), preferred_element_type=F32
        )
        w_score[...] = (wide * (1.0 / math.sqrt(channels))).astype(BF16)
        w_mixed[...] = matmul(wv[...], wo[...]).astype(BF16)


    def attend(half, copies, cols_row):
        for copy in copies:
            copy.wait_recv()

        @stage
        def _():
            here = moved.at[half]
            groups = [slice(g * GROUP, (g + 1) * GROUP) for g in range(slots // GROUP)]
            residual, queries, values, scores = [], [], [], []
            for part in groups:
                taps = [
                    matmul(here[tap : tap + frame_count, part].reshape(span, channels), tk[tap])
                    for tap in range(3)
                ]
                centre = here[1 : 1 + frame_count, part].reshape(span, channels).astype(F32)
                residual.append((centre + taps[0] + taps[1] + taps[2]).astype(BF16).astype(F32))
            gained = [(widened * gain_ref[...]).astype(BF16) for widened in residual]
            for r in gained:
                queries.append(matmul(r, w_score[...]).astype(BF16))
            scales = [
                lax.rsqrt(jnp.mean(widened * widened, axis=-1, keepdims=True) + 1e-06)
                for widened in residual
            ]
            keys = [
                (widened * scale * gain_ref[...]).astype(BF16)
                for widened, scale in zip(residual, scales)
            ]
            for r, scale in zip(gained, scales):
                values.append((matmul(r, w_mixed[...]) * scale).astype(BF16))
            for q, k in zip(queries, keys):
                scores.append(
                    lax.dot_general(
                        q, k, (((1,), (1,)), ((), ())), preferred_element_type=F32
                    )
                )
            scores = [
                score * scale + masked_bias[...] for score, scale in zip(scores, scales)
            ]
            peaks = [jnp.max(score, axis=-1, keepdims=True) for score in scores]
            raised = [jnp.exp(score - peak) for score, peak in zip(scores, peaks)]
            totals = [1.0 / jnp.sum(r, axis=-1, keepdims=True) for r in raised]
            parts = []
            for r, t, v, w in zip(raised, totals, values, residual):
                mixed = w + matmul(r.astype(BF16), v) * t
                parts.append(mixed.reshape(frame_count, GROUP, channels))
            attended = jnp.concatenate(parts, axis=1)
            outer = attended[:, inner : inner + cols]
            place = lax.broadcasted_iota(jnp.int32, outer.shape, 1)
            for j in range(half_rows):
                here = attended[:, j * cols : (j + 1) * cols]
                edge_pair = pltpu.roll(outer, (cols - 1 - 2 * j) % cols, 1)
                left = pltpu.roll(jnp.where(place == cols - 1, edge_pair, here), 1, 1)
                right = pltpu.roll(jnp.where(place == 0, edge_pair, here), cols - 1, 1)
                for b, part in enumerate((left, here, right)):
                    cols3[cols_row + j, :, b * channels : (b + 1) * channels] = part.reshape(
                        frame_count * cols, channels
                    ).astype(BF16)

    def third(rows, a):
        part = matmul(rows.reshape(-1, 3 * channels), w3[mirrored(a, 3)].reshape(3 * channels, channels))
        return part.reshape(-1, frame_count, cols, channels)

    attend(1, near_copies, half_rows)
    for copy in w3_loads:
        copy.wait()

    def near_third():
        two = third(cols3[half_rows : n + 2], 2)
        one = third(cols3[half_rows : n + 1], 1)
        zero = third(cols3[half_rows:n], 0)
        partial3[0] = two[0]
        partial3[1] = two[1] + one[0]
        out_ref[:, mirrored(n - 1, n)] = (two[2] + one[1] + zero[0]).astype(BF16)

    def far_third():
        zero = third(cols3[0:half_rows], 0)
        one = third(cols3[1:half_rows], 1)
        two = third(cols3[2:half_rows], 2)
        out_ref[:, mirrored(0, n)] = (zero[0] + one[0] + two[0]).astype(BF16)
        out_ref[:, mirrored(1, n)] = (partial3[0] + zero[1] + one[1]).astype(BF16)
        out_ref[:, mirrored(2, n)] = (partial3[1] + zero[2]).astype(BF16)

    def whole_third():
        sums = [third(cols3[a : a + n], a) for a in range(3)]
        summed = sums[0] + sums[1] + sums[2]
        for t in range(n):
            out_ref[:, mirrored(t, n)] = summed[t].astype(BF16)

    stage(near_third, others)
    attend(0, far_copies, 0)
    stage(far_third, others)
    stage(whole_third, 1 - others)

    pl.when(has_far)(to_far.wait_send)
    to_near.wait_send()
    for copy in near_copies + far_copies:
        copy.wait_send()


def on_device(frames_axis, rows_axis, *args):
    frames_in = args[0]
    norm_gain = args[4]
    local_frames, n, width, channels = frames_in.shape
    frame_count = local_frames * frames_axis
    cols = width // frames_axis
    half_rows = (n + 2) // 2
    slots = -(-half_rows * (cols + 2) // GROUP) * GROUP
    args = args[:4] + (norm_gain.reshape(1, channels),) + args[5:]
    any_space = pl.BlockSpec(memory_space=pl.ANY)
    vmem = pl.BlockSpec(memory_space=pltpu.VMEM)
    weight = pltpu.VMEM((3, 3, channels, channels), BF16)
    square = pltpu.VMEM((channels, channels), BF16)
    halo = pltpu.VMEM((local_frames, HALO, width, channels), BF16)
    return pl.pallas_call(
        functools.partial(kernel, frames_axis, rows_axis),
        out_shape=pltpu.VMEM((frame_count, n, cols, channels), BF16),
        in_specs=[any_space] * 11,
        out_specs=vmem,
        scratch_shapes=[
            pltpu.VMEM((local_frames, n, width, channels), BF16),
            halo,
            halo,
            pltpu.VMEM((local_frames, n + 2 * HALO, width, 3 * channels), BF16),
            pltpu.VMEM((local_frames, n + 4, width, 3 * channels), BF16),
            weight,
            weight,
            pltpu.VMEM((3, channels, channels), BF16),
            square,
            square,
            square,
            square,
            weight,
            pltpu.VMEM((local_frames, 4, width, channels), F32),
            pltpu.VMEM((2, frame_count, cols, channels), F32),
            pltpu.VMEM((1, channels), F32),
            pltpu.VMEM((frame_count, frame_count), F32),
            pltpu.VMEM((2, frames_axis, local_frames, slots, channels), BF16),
            pltpu.VMEM((2, frame_count + 2, slots, channels), BF16),
            pltpu.VMEM((frame_count * GROUP, frame_count * GROUP), F32),
            square,
            square,
            pltpu.VMEM((n + 2, frame_count * cols, 3 * channels), BF16),
            pltpu.SemaphoreType.DMA((11,)),
            pltpu.SemaphoreType.REGULAR,
            pltpu.SemaphoreType.REGULAR,
            pltpu.SemaphoreType.REGULAR,
            pltpu.SemaphoreType.DMA((2,)),
            pltpu.SemaphoreType.DMA((2,)),
            pltpu.SemaphoreType.DMA((2, frames_axis)),
            pltpu.SemaphoreType.DMA((2, frames_axis)),
        ],
        compiler_params=pltpu.CompilerParams(
            collective_id=0, has_side_effects=True, vmem_limit_bytes=56 * 1024 * 1024
        ),
    )(*args)


def solution(mesh):
    placed = (P("frame", "row", None, None),) + (P(),) * 10
    return jax.shard_map(
        functools.partial(on_device, mesh.shape["frame"], mesh.shape["row"]),
        mesh=mesh,
        in_specs=placed,
        out_specs=P(None, "row", "frame", None),
        check_vma=False,
    )
```

```python
import functools
import math

import jax
import jax.numpy as jnp
from jax import lax
from jax.experimental import pallas as pl
from jax.experimental.pallas import tpu as pltpu
from jax.sharding import PartitionSpec as P

MESH = pl.DeviceIdType.MESH
BF16 = jnp.bfloat16
F32 = jnp.float32
HALO = 3
GROUP = 16


def matmul(lhs, rhs):
    return jnp.dot(lhs, rhs, preferred_element_type=F32)


def partner(index, distance, count):
    if count & (count - 1):
        return lax.rem(index + distance, count)
    bit = 1
    while bit < count:
        if distance & bit:
            index = index + bit - 2 * bit * lax.rem(lax.div(index, bit), 2)
        bit *= 2
    return index


def silu(v):
    half = 0.5 * v
    return half + half * jnp.tanh(half)


def silu_of_sum(one, two):
    half = 0.5 * one + 0.5 * two
    return half + half * jnp.tanh(half)


def steps_below(index, pitch, count):
    quotient = jnp.zeros_like(index)
    for k in range(1, count):
        quotient = quotient + (index >= k * pitch).astype(jnp.int32)
    return quotient


def shifted_columns(rows, width):
    count, _, channels = rows.shape
    flat = rows.astype(F32).reshape(count * width, channels)
    column = lax.broadcasted_iota(jnp.int32, (count, width, channels), 1)
    left = pltpu.roll(flat, 1, 0).reshape(count, width, channels)
    right = pltpu.roll(flat, count * width - 1, 0).reshape(count, width, channels)
    left = jnp.where(column == 0, 0.0, left).astype(BF16)
    right = jnp.where(column == width - 1, 0.0, right).astype(BF16)
    return left, right


def spread(dst, first_row, rows, width):
    count, _, channels = rows.shape
    left, right = shifted_columns(rows, width)
    span = slice(first_row, first_row + count)
    dst[span, :, 0:channels] = left
    dst[span, :, channels : 2 * channels] = rows
    dst[span, :, 2 * channels : 3 * channels] = right


def kernel(
    frames_axis,
    rows_axis,
    x_hbm,
    w1_hbm,
    w2_hbm,
    tk_hbm,
    gain_hbm,
    wq_hbm,
    wk_hbm,
    wv_hbm,
    wo_hbm,
    bias_hbm,
    w3_hbm,
    out_ref,
    xin,
    far_in,
    near_in,
    xs,
    fs,
    w1,
    w2,
    tk,
    wq,
    wk,
    wv,
    wo,
    w3,
    partial,
    partial3,
    gain_ref,
    bias_ref,
    packed,
    moved,
    masked_bias,
    w_score,
    w_mixed,
    cols3,
    load_sem,
    near_sem,
    peer_sem,
    go_sem,
    halo_send,
    halo_recv,
    send_sem,
    recv_sem,
):
    frame = lax.axis_index("frame")
    row = lax.axis_index("row")
    local_frames, n, width, channels = x_hbm.shape
    frame_count = frames_axis * local_frames
    cols = width // frames_axis
    half_rows = (n + 2) // 2
    slots = packed.shape[3]

    odd = lax.rem(row, 2)
    near = row + 1 - 2 * odd
    far = lax.rem(row - 1 + 2 * odd + rows_axis, rows_axis)
    has_far = (row + odd > 0) & (row + odd < rows_axis)

    once = 1 + lax.div(frame, frames_axis)

    def stage(body, wanted=None):
        steps = once if wanted is None else once * wanted
        lax.fori_loop(0, steps, lambda _, carry: (body(), carry)[1], 0)

    barrier = pltpu.get_barrier_semaphore()
    peers = [lax.rem(frame + k, frames_axis) for k in range(1, frames_axis)]
    others = has_far.astype(jnp.int32)

    def signal(semaphore, **place):
        pl.semaphore_signal(semaphore, inc=1, device_id=place, device_id_type=MESH)

    @pl.when(has_far)
    def _():
        signal(barrier, row=far)

    @pl.when(odd == 1)
    def _():
        signal(barrier, row=near)
        for peer in peers:
            signal(barrier, frame=peer)

    def halo(side, source):
        far_side = side == 0
        from_top = odd if far_side else 1 - odd
        return pltpu.make_async_remote_copy(
            src_ref=source.at[:, pl.ds(from_top * (n - HALO), HALO)],
            dst_ref=far_in if far_side else near_in,
            send_sem=halo_send.at[side],
            recv_sem=halo_recv.at[side],
            device_id={"row": far if far_side else near},
            device_id_type=MESH,
        )

    to_far, to_near = halo(0, xin), halo(1, xin)

    count = [0]

    def load(src, dst):
        copy = pltpu.make_async_copy(src, dst, load_sem.at[count[0]])
        count[0] += 1
        return copy

    def mirrored(i, size):
        return i + odd * (size - 1 - 2 * i)

    x_loads = [load(x_hbm, xin)]
    w1_loads = [load(w1_hbm, w1)]
    w2_loads = [load(w2_hbm, w2)]
    late_loads = [
        load(src, dst)
        for src, dst in (
            (tk_hbm, tk),
            (gain_hbm, gain_ref),
            (wq_hbm, wq),
            (wk_hbm, wk),
            (wv_hbm, wv),
            (bias_hbm, bias_ref),
            (wo_hbm, wo),
        )
    ]
    w3_loads = [load(w3_hbm, w3)]
    for copy in x_loads:
        copy.start()
    all_loads = w1_loads + w2_loads + late_loads + w3_loads

    def start_loads():
        for copy in all_loads:
            copy.start()

    halo_first = has_far & (odd == 0)
    pl.when(jnp.logical_not(halo_first))(start_loads)

    @pl.when(odd == 0)
    def _():
        pl.semaphore_wait(barrier, others + 1)
        signal(near_sem, row=near)
        pl.when(has_far)(halo(0, x_hbm).start)

    pl.when(halo_first)(start_loads)
    for copy in x_loads:
        copy.wait()
    pl.when(odd == 0)(to_near.start)

    @pl.when(odd == 1)
    def _():
        pl.semaphore_wait(near_sem, 1)
        to_near.start()
        pl.semaphore_wait(barrier, others + frames_axis - 1)
        pl.when(has_far)(to_far.start)
        for peer in peers:
            signal(peer_sem, frame=peer)

    inner = half_rows * cols
    edge = jnp.zeros((2, 1, slots, channels), BF16)
    moved[:, 0:1] = edge
    moved[:, frame_count + 1 : frame_count + 2] = edge

    for f in range(local_frames):
        spread(xs.at[f], HALO, jnp.stack([xin[f, mirrored(t, n)] for t in range(n)]), width)
    for copy in w1_loads:
        copy.wait()
    def edges(rows, a):
        part = matmul(
            rows.reshape(-1, 3 * channels), w1[mirrored(a, 3)].reshape(3 * channels, channels)
        )
        return part.reshape(local_frames, -1, width, channels)

    @stage
    def _():
        zero = edges(xs[:, HALO : HALO + n], 0)
        one = edges(xs[:, HALO + 1 : HALO + n], 1)
        two = edges(xs[:, HALO + 2 : HALO + n], 2)
        partial[:, 2] = zero[:, n - 2] + one[:, n - 2]
        partial[:, 3] = zero[:, n - 1]
        for f in range(local_frames):
            whole = [zero[f, t] + one[f, t] + two[f, t] for t in range(n - 2)]
            spread(fs.at[f], 3, silu(jnp.stack(whole)).astype(BF16), width)

    def pack(half, second):
        none = jnp.zeros((local_frames, cols, channels), F32)
        place = lax.broadcasted_iota(jnp.int32, none.shape, 1)
        blocks = [
            [second[:, j, o * cols : (o + 1) * cols] for j in range(half_rows)]
            for o in range(frames_axis)
        ]
        for o in range(frames_axis):
            outer = none
            for side, (p, at) in enumerate(((o - 1, cols - 1), (o + 1, 0))):
                if not 0 <= p < frames_axis:
                    continue
                for j in range(half_rows):
                    to = 2 * j + side
                    turned = pltpu.roll(blocks[p][j], (to - at) % cols, 1)
                    outer = jnp.where(place == to, turned, outer)
            packed[half, o] = jnp.concatenate([*blocks[o], outer], axis=1).astype(BF16)

    def second_half(half, first_row):
        @stage
        def _():
            def rows(a, k):
                taken = fs[:, first_row + a : first_row + a + half_rows, :, k : k + channels]
                return taken.reshape(-1, channels)

            taps = [(a, k * channels) for a in range(3) for k in range(3)]
            cut = (len(taps) + 1) // 2
            sums = []
            for some in (taps[:cut], taps[cut:]):
                total = None
                for a, k in some:
                    part = matmul(rows(a, k), w2[mirrored(a, 3)].reshape(3 * channels, channels)[k : k + channels])
                    total = part if total is None else total + part
                sums.append(total)
            second = silu_of_sum(*sums).reshape(local_frames, half_rows, width, channels)
            if half == 0:
                place = lax.broadcasted_iota(jnp.int32, second.shape, 1)
                second = jnp.where((place > 0) | has_far, second, 0.0)
            pack(half, second)

        copies = []
        if half == 1:

            @pl.when(odd == 0)
            def _():
                pl.semaphore_wait(go_sem, 1)

        place = pl.ds(1 + frame * local_frames, local_frames)
        for k in reversed(range(1, frames_axis)):
            peer = partner(frame, k, frames_axis)
            copy = pltpu.make_async_remote_copy(
                src_ref=packed.at[half, peer],
                dst_ref=moved.at[half, place],
                send_sem=send_sem.at[half, k],
                recv_sem=recv_sem.at[half, k],
                device_id={"frame": peer},
                device_id_type=MESH,
            )
            copy.start()
            copies.append(copy)
        moved[half, place] = packed[half, frame]
        return copies

    to_near.wait_recv()

    @stage
    def _():
        for f in range(local_frames):
            spread(
                xs.at[f],
                HALO + n,
                jnp.stack([near_in[f, j + odd * (HALO - 1 - 2 * j)] for j in range(HALO)]),
                width,
            )
        top = HALO + n
        two = edges(xs[:, top : top + 3], 2)
        one = edges(xs[:, top : top + 2], 1)
        zero = edges(xs[:, top : top + 1], 0)
        for f in range(local_frames):
            rows = jnp.stack(
                [
                    partial[f, 2] + two[f, 0],
                    partial[f, 3] + two[f, 1] + one[f, 0],
                    two[f, 2] + one[f, 1] + zero[f, 0],
                ]
            )
            spread(fs.at[f], n + 1, silu(rows).astype(BF16), width)

    for copy in w2_loads:
        copy.wait()

    @pl.when(odd == 1)
    def _():
        pl.semaphore_wait(peer_sem, frames_axis - 1)
        signal(go_sem, row=near)

    near_copies = second_half(1, half_rows)

    @stage
    def _():
        one = edges(xs[:, HALO : HALO + 1], 1)
        two = edges(xs[:, HALO : HALO + 2], 2)
        partial[:, 0] = two[:, 0]
        partial[:, 1] = one[:, 0] + two[:, 1]

    pl.when(has_far)(to_far.wait_recv)

    def far_edges():
        for f in range(local_frames):
            spread(
                xs.at[f], 0, jnp.stack([far_in[f, j + odd * (HALO - 1 - 2 * j)] for j in range(HALO)]), width
            )
        zero = edges(xs[:, 0:3], 0)
        one = edges(xs[:, 1:3], 1)
        two = edges(xs[:, 2:3], 2)
        for f in range(local_frames):
            rows = jnp.stack(
                [
                    zero[f, 0] + one[f, 0] + two[f, 0],
                    partial[f, 0] + zero[f, 1] + one[f, 1],
                    partial[f, 1] + zero[f, 2],
                ]
            )
            rows = silu(rows)
            spread(fs.at[f], 0, rows.astype(BF16), width)

    def no_far_edges():
        for f in range(local_frames):
            last = silu(partial[f, 1])
            rows = jnp.stack([jnp.zeros_like(last), jnp.zeros_like(last), last])
            spread(fs.at[f], 0, rows.astype(BF16), width)

    stage(far_edges, others)
    stage(no_far_edges, 1 - others)
    far_copies = second_half(0, 0)

    for copy in late_loads:
        copy.wait()
    span = frame_count * GROUP
    lane = lax.broadcasted_iota(jnp.int32, (frame_count, span), 1)
    wide = jnp.zeros((frame_count, span), F32)
    for g in range(frame_count):
        inside = (lane >= g * GROUP) & (lane < (g + 1) * GROUP)
        wide = jnp.where(inside, bias_ref[:, g : g + 1], wide)
    wide = jnp.broadcast_to(wide[:, None, :], (frame_count, GROUP, span)).reshape(span, span)
    query_pixel = jnp.bitwise_and(lax.broadcasted_iota(jnp.int32, (span, span), 0), GROUP - 1)
    key_pixel = jnp.bitwise_and(lax.broadcasted_iota(jnp.int32, (span, span), 1), GROUP - 1)
    masked_bias[...] = jnp.where(query_pixel == key_pixel, wide, -1e30)

    @stage
    def _():
        wide = lax.dot_general(
            wq[...], wk[...], (((1,), (1,)), ((), ())), preferred_element_type=F32
        )
        w_score[...] = (wide * (1.0 / math.sqrt(channels))).astype(BF16)
        w_mixed[...] = matmul(wv[...], wo[...]).astype(BF16)


    def attend(half, copies, cols_row):
        for copy in copies:
            copy.wait_recv()

        @stage
        def _():
            here = moved.at[half]
            groups = [slice(g * GROUP, (g + 1) * GROUP) for g in range(slots // GROUP)]
            residual, queries, values, scores = [], [], [], []
            for part in groups:
                taps = [
                    matmul(here[tap : tap + frame_count, part].reshape(span, channels), tk[tap])
                    for tap in range(3)
                ]
                centre = here[1 : 1 + frame_count, part].reshape(span, channels).astype(F32)
                residual.append((centre + taps[0] + taps[1] + taps[2]).astype(BF16).astype(F32))
            gained = [(widened * gain_ref[...]).astype(BF16) for widened in residual]
            for r in gained:
                queries.append(matmul(r, w_score[...]).astype(BF16))
            scales = [
                lax.rsqrt(jnp.mean(widened * widened, axis=-1, keepdims=True) + 1e-06)
                for widened in residual
            ]
            keys = [
                (widened * scale * gain_ref[...]).astype(BF16)
                for widened, scale in zip(residual, scales)
            ]
            for r, scale in zip(gained, scales):
                values.append((matmul(r, w_mixed[...]) * scale).astype(BF16))
            for q, k in zip(queries, keys):
                scores.append(
                    lax.dot_general(
                        q, k, (((1,), (1,)), ((), ())), preferred_element_type=F32
                    )
                )
            scores = [
                score * scale + masked_bias[...] for score, scale in zip(scores, scales)
            ]
            peaks = [jnp.max(score, axis=-1, keepdims=True) for score in scores]
            raised = [jnp.exp(score - peak) for score, peak in zip(scores, peaks)]
            totals = [1.0 / jnp.sum(r, axis=-1, keepdims=True) for r in raised]
            parts = []
            for r, t, v, w in zip(raised, totals, values, residual):
                mixed = w + matmul(r.astype(BF16), v) * t
                parts.append(mixed.reshape(frame_count, GROUP, channels))
            attended = jnp.concatenate(parts, axis=1)
            outer = attended[:, inner : inner + cols]
            place = lax.broadcasted_iota(jnp.int32, outer.shape, 1)
            for j in range(half_rows):
                here = attended[:, j * cols : (j + 1) * cols]
                edge_pair = pltpu.roll(outer, (cols - 1 - 2 * j) % cols, 1)
                left = pltpu.roll(jnp.where(place == cols - 1, edge_pair, here), 1, 1)
                right = pltpu.roll(jnp.where(place == 0, edge_pair, here), cols - 1, 1)
                for b, part in enumerate((left, here, right)):
                    cols3[cols_row + j, :, b * channels : (b + 1) * channels] = part.reshape(
                        frame_count * cols, channels
                    ).astype(BF16)

    def third(rows, a):
        part = matmul(rows.reshape(-1, 3 * channels), w3[mirrored(a, 3)].reshape(3 * channels, channels))
        return part.reshape(-1, frame_count, cols, channels)

    attend(1, near_copies, half_rows)
    for copy in w3_loads:
        copy.wait()

    def near_third():
        two = third(cols3[half_rows : n + 2], 2)
        one = third(cols3[half_rows : n + 1], 1)
        zero = third(cols3[half_rows:n], 0)
        partial3[0] = two[0]
        partial3[1] = two[1] + one[0]
        out_ref[:, mirrored(n - 1, n)] = (two[2] + one[1] + zero[0]).astype(BF16)

    def far_third():
        zero = third(cols3[0:half_rows], 0)
        one = third(cols3[1:half_rows], 1)
        two = third(cols3[2:half_rows], 2)
        out_ref[:, mirrored(0, n)] = (zero[0] + one[0] + two[0]).astype(BF16)
        out_ref[:, mirrored(1, n)] = (partial3[0] + zero[1] + one[1]).astype(BF16)
        out_ref[:, mirrored(2, n)] = (partial3[1] + zero[2]).astype(BF16)

    def whole_third():
        sums = [third(cols3[a : a + n], a) for a in range(3)]
        summed = sums[0] + sums[1] + sums[2]
        for t in range(n):
            out_ref[:, mirrored(t, n)] = summed[t].astype(BF16)

    stage(near_third, others)
    attend(0, far_copies, 0)
    stage(far_third, others)
    stage(whole_third, 1 - others)

    pl.when(has_far)(to_far.wait_send)
    to_near.wait_send()
    for copy in near_copies + far_copies:
        copy.wait_send()


def on_device(frames_axis, rows_axis, *args):
    frames_in = args[0]
    norm_gain = args[4]
    local_frames, n, width, channels = frames_in.shape
    frame_count = local_frames * frames_axis
    cols = width // frames_axis
    half_rows = (n + 2) // 2
    slots = -(-half_rows * (cols + 2) // GROUP) * GROUP
    args = args[:4] + (norm_gain.reshape(1, channels),) + args[5:]
    any_space = pl.BlockSpec(memory_space=pl.ANY)
    vmem = pl.BlockSpec(memory_space=pltpu.VMEM)
    weight = pltpu.VMEM((3, 3, channels, channels), BF16)
    square = pltpu.VMEM((channels, channels), BF16)
    halo = pltpu.VMEM((local_frames, HALO, width, channels), BF16)
    return pl.pallas_call(
        functools.partial(kernel, frames_axis, rows_axis),
        out_shape=pltpu.VMEM((frame_count, n, cols, channels), BF16),
        in_specs=[any_space] * 11,
        out_specs=vmem,
        scratch_shapes=[
            pltpu.VMEM((local_frames, n, width, channels), BF16),
            halo,
            halo,
            pltpu.VMEM((local_frames, n + 2 * HALO, width, 3 * channels), BF16),
            pltpu.VMEM((local_frames, n + 4, width, 3 * channels), BF16),
            weight,
            weight,
            pltpu.VMEM((3, channels, channels), BF16),
            square,
            square,
            square,
            square,
            weight,
            pltpu.VMEM((local_frames, 4, width, channels), F32),
            pltpu.VMEM((2, frame_count, cols, channels), F32),
            pltpu.VMEM((1, channels), F32),
            pltpu.VMEM((frame_count, frame_count), F32),
            pltpu.VMEM((2, frames_axis, local_frames, slots, channels), BF16),
            pltpu.VMEM((2, frame_count + 2, slots, channels), BF16),
            pltpu.VMEM((frame_count * GROUP, frame_count * GROUP), F32),
            square,
            square,
            pltpu.VMEM((n + 2, frame_count * cols, 3 * channels), BF16),
            pltpu.SemaphoreType.DMA((11,)),
            pltpu.SemaphoreType.REGULAR,
            pltpu.SemaphoreType.REGULAR,
            pltpu.SemaphoreType.REGULAR,
            pltpu.SemaphoreType.DMA((2,)),
            pltpu.SemaphoreType.DMA((2,)),
            pltpu.SemaphoreType.DMA((2, frames_axis)),
            pltpu.SemaphoreType.DMA((2, frames_axis)),
        ],
        compiler_params=pltpu.CompilerParams(
            collective_id=0, has_side_effects=True, vmem_limit_bytes=56 * 1024 * 1024
        ),
    )(*args)


def solution(mesh):
    placed = (P("frame", "row", None, None),) + (P(),) * 10
    return jax.shard_map(
        functools.partial(on_device, mesh.shape["frame"], mesh.shape["row"]),
        mesh=mesh,
        in_specs=placed,
        out_specs=P(None, "row", "frame", None),
        check_vma=False,
    )
```

```python
import functools
import math

import jax
import jax.numpy as jnp
from jax import lax
from jax.experimental import pallas as pl
from jax.experimental.pallas import tpu as pltpu
from jax.sharding import PartitionSpec as P

MESH = pl.DeviceIdType.MESH
BF16 = jnp.bfloat16
F32 = jnp.float32
HALO = 3
GROUP = 16


def matmul(lhs, rhs):
    return jnp.dot(lhs, rhs, preferred_element_type=F32)


def partner(index, distance, count):
    if count & (count - 1):
        return lax.rem(index + distance, count)
    bit = 1
    while bit < count:
        if distance & bit:
            index = index + bit - 2 * bit * lax.rem(lax.div(index, bit), 2)
        bit *= 2
    return index


def silu(v):
    half = 0.5 * v
    return half + half * jnp.tanh(half)


def silu_of_sum(one, two):
    half = 0.5 * one + 0.5 * two
    return half + half * jnp.tanh(half)


def steps_below(index, pitch, count):
    quotient = jnp.zeros_like(index)
    for k in range(1, count):
        quotient = quotient + (index >= k * pitch).astype(jnp.int32)
    return quotient


def shifted_columns(rows, width):
    count, _, channels = rows.shape
    flat = rows.astype(F32).reshape(count * width, channels)
    column = lax.broadcasted_iota(jnp.int32, (count, width, channels), 1)
    left = pltpu.roll(flat, 1, 0).reshape(count, width, channels)
    right = pltpu.roll(flat, count * width - 1, 0).reshape(count, width, channels)
    left = jnp.where(column == 0, 0.0, left).astype(BF16)
    right = jnp.where(column == width - 1, 0.0, right).astype(BF16)
    return left, right


def spread(dst, first_row, rows, width):
    count, _, channels = rows.shape
    left, right = shifted_columns(rows, width)
    span = slice(first_row, first_row + count)
    dst[span, :, 0:channels] = left
    dst[span, :, channels : 2 * channels] = rows
    dst[span, :, 2 * channels : 3 * channels] = right


def kernel(
    frames_axis,
    rows_axis,
    x_hbm,
    w1_hbm,
    w2_hbm,
    tk_hbm,
    gain_hbm,
    wq_hbm,
    wk_hbm,
    wv_hbm,
    wo_hbm,
    bias_hbm,
    w3_hbm,
    out_ref,
    xin,
    far_in,
    near_in,
    xs,
    fs,
    w1,
    w2,
    tk,
    wq,
    wk,
    wv,
    wo,
    w3,
    partial,
    partial3,
    gain_ref,
    bias_ref,
    packed,
    moved,
    masked_bias,
    w_score,
    w_mixed,
    cols3,
    load_sem,
    near_sem,
    peer_sem,
    go_sem,
    halo_send,
    halo_recv,
    send_sem,
    recv_sem,
):
    frame = lax.axis_index("frame")
    row = lax.axis_index("row")
    local_frames, n, width, channels = x_hbm.shape
    frame_count = frames_axis * local_frames
    cols = width // frames_axis
    half_rows = (n + 2) // 2
    slots = packed.shape[3]

    odd = lax.rem(row, 2)
    near = row + 1 - 2 * odd
    far = lax.rem(row - 1 + 2 * odd + rows_axis, rows_axis)
    has_far = (row + odd > 0) & (row + odd < rows_axis)

    once = 1 + lax.div(frame, frames_axis)

    def stage(body, wanted=None):
        steps = once if wanted is None else once * wanted
        lax.fori_loop(0, steps, lambda _, carry: (body(), carry)[1], 0)

    barrier = pltpu.get_barrier_semaphore()
    peers = [lax.rem(frame + k, frames_axis) for k in range(1, frames_axis)]
    others = has_far.astype(jnp.int32)

    def signal(semaphore, **place):
        pl.semaphore_signal(semaphore, inc=1, device_id=place, device_id_type=MESH)

    @pl.when(has_far)
    def _():
        signal(barrier, row=far)

    @pl.when(odd == 1)
    def _():
        signal(barrier, row=near)
        for peer in peers:
            signal(barrier, frame=peer)

    def halo(side, source):
        far_side = side == 0
        from_top = odd if far_side else 1 - odd
        return pltpu.make_async_remote_copy(
            src_ref=source.at[:, pl.ds(from_top * (n - HALO), HALO)],
            dst_ref=far_in if far_side else near_in,
            send_sem=halo_send.at[side],
            recv_sem=halo_recv.at[side],
            device_id={"row": far if far_side else near},
            device_id_type=MESH,
        )

    to_far, to_near = halo(0, xin), halo(1, xin)

    count = [0]

    def load(src, dst):
        copy = pltpu.make_async_copy(src, dst, load_sem.at[count[0]])
        count[0] += 1
        return copy

    def mirrored(i, size):
        return i + odd * (size - 1 - 2 * i)

    x_loads = [load(x_hbm, xin)]
    w1_loads = [load(w1_hbm, w1)]
    w2_loads = [load(w2_hbm, w2)]
    late_loads = [
        load(src, dst)
        for src, dst in (
            (tk_hbm, tk),
            (gain_hbm, gain_ref),
            (wq_hbm, wq),
            (wk_hbm, wk),
            (wv_hbm, wv),
            (bias_hbm, bias_ref),
            (wo_hbm, wo),
        )
    ]
    w3_loads = [load(w3_hbm, w3)]
    for copy in x_loads:
        copy.start()

    def start_loads():
        for copy in w1_loads:
            copy.start()
        for copy in w2_loads + late_loads + w3_loads:
            copy.start(priority=1)

    halo_first = has_far & (odd == 0)
    pl.when(jnp.logical_not(halo_first))(start_loads)

    @pl.when(odd == 0)
    def _():
        pl.semaphore_wait(barrier, others + 1)
        signal(near_sem, row=near)
        pl.when(has_far)(halo(0, x_hbm).start)

    pl.when(halo_first)(start_loads)
    for copy in x_loads:
        copy.wait()
    pl.when(odd == 0)(to_near.start)

    @pl.when(odd == 1)
    def _():
        pl.semaphore_wait(near_sem, 1)
        to_near.start()
        pl.semaphore_wait(barrier, others + frames_axis - 1)
        pl.when(has_far)(to_far.start)
        for peer in peers:
            signal(peer_sem, frame=peer)

    inner = half_rows * cols
    edge = jnp.zeros((2, 1, slots, channels), BF16)
    moved[:, 0:1] = edge
    moved[:, frame_count + 1 : frame_count + 2] = edge

    for f in range(local_frames):
        spread(xs.at[f], HALO, jnp.stack([xin[f, mirrored(t, n)] for t in range(n)]), width)
    for copy in w1_loads:
        copy.wait()
    def edges(rows, a):
        part = matmul(
            rows.reshape(-1, 3 * channels), w1[mirrored(a, 3)].reshape(3 * channels, channels)
        )
        return part.reshape(local_frames, -1, width, channels)

    @stage
    def _():
        zero = edges(xs[:, HALO : HALO + n], 0)
        one = edges(xs[:, HALO + 1 : HALO + n], 1)
        two = edges(xs[:, HALO + 2 : HALO + n], 2)
        partial[:, 2] = zero[:, n - 2] + one[:, n - 2]
        partial[:, 3] = zero[:, n - 1]
        for f in range(local_frames):
            whole = [zero[f, t] + one[f, t] + two[f, t] for t in range(n - 2)]
            spread(fs.at[f], 3, silu(jnp.stack(whole)).astype(BF16), width)

    def pack(half, second):
        none = jnp.zeros((local_frames, cols, channels), F32)
        place = lax.broadcasted_iota(jnp.int32, none.shape, 1)
        blocks = [
            [second[:, j, o * cols : (o + 1) * cols] for j in range(half_rows)]
            for o in range(frames_axis)
        ]
        for o in range(frames_axis):
            outer = none
            for side, (p, at) in enumerate(((o - 1, cols - 1), (o + 1, 0))):
                if not 0 <= p < frames_axis:
                    continue
                for j in range(half_rows):
                    to = 2 * j + side
                    turned = pltpu.roll(blocks[p][j], (to - at) % cols, 1)
                    outer = jnp.where(place == to, turned, outer)
            packed[half, o] = jnp.concatenate([*blocks[o], outer], axis=1).astype(BF16)

    def second_half(half, first_row):
        @stage
        def _():
            def rows(a, k):
                taken = fs[:, first_row + a : first_row + a + half_rows, :, k : k + channels]
                return taken.reshape(-1, channels)

            taps = [(a, k * channels) for a in range(3) for k in range(3)]
            cut = (len(taps) + 1) // 2
            sums = []
            for some in (taps[:cut], taps[cut:]):
                total = None
                for a, k in some:
                    part = matmul(rows(a, k), w2[mirrored(a, 3)].reshape(3 * channels, channels)[k : k + channels])
                    total = part if total is None else total + part
                sums.append(total)
            second = silu_of_sum(*sums).reshape(local_frames, half_rows, width, channels)
            if half == 0:
                place = lax.broadcasted_iota(jnp.int32, second.shape, 1)
                second = jnp.where((place > 0) | has_far, second, 0.0)
            pack(half, second)

        copies = []
        if half == 1:

            @pl.when(odd == 0)
            def _():
                pl.semaphore_wait(go_sem, 1)

        place = pl.ds(1 + frame * local_frames, local_frames)
        for k in reversed(range(1, frames_axis)):
            peer = partner(frame, k, frames_axis)
            copy = pltpu.make_async_remote_copy(
                src_ref=packed.at[half, peer],
                dst_ref=moved.at[half, place],
                send_sem=send_sem.at[half, k],
                recv_sem=recv_sem.at[half, k],
                device_id={"frame": peer},
                device_id_type=MESH,
            )
            copy.start()
            copies.append(copy)
        moved[half, place] = packed[half, frame]
        return copies

    to_near.wait_recv()

    @stage
    def _():
        for f in range(local_frames):
            spread(
                xs.at[f],
                HALO + n,
                jnp.stack([near_in[f, j + odd * (HALO - 1 - 2 * j)] for j in range(HALO)]),
                width,
            )
        top = HALO + n
        two = edges(xs[:, top : top + 3], 2)
        one = edges(xs[:, top : top + 2], 1)
        zero = edges(xs[:, top : top + 1], 0)
        for f in range(local_frames):
            rows = jnp.stack(
                [
                    partial[f, 2] + two[f, 0],
                    partial[f, 3] + two[f, 1] + one[f, 0],
                    two[f, 2] + one[f, 1] + zero[f, 0],
                ]
            )
            spread(fs.at[f], n + 1, silu(rows).astype(BF16), width)

    for copy in w2_loads:
        copy.wait()

    @pl.when(odd == 1)
    def _():
        pl.semaphore_wait(peer_sem, frames_axis - 1)
        signal(go_sem, row=near)

    near_copies = second_half(1, half_rows)

    @stage
    def _():
        one = edges(xs[:, HALO : HALO + 1], 1)
        two = edges(xs[:, HALO : HALO + 2], 2)
        partial[:, 0] = two[:, 0]
        partial[:, 1] = one[:, 0] + two[:, 1]

    pl.when(has_far)(to_far.wait_recv)

    def far_edges():
        for f in range(local_frames):
            spread(
                xs.at[f], 0, jnp.stack([far_in[f, j + odd * (HALO - 1 - 2 * j)] for j in range(HALO)]), width
            )
        zero = edges(xs[:, 0:3], 0)
        one = edges(xs[:, 1:3], 1)
        two = edges(xs[:, 2:3], 2)
        for f in range(local_frames):
            rows = jnp.stack(
                [
                    zero[f, 0] + one[f, 0] + two[f, 0],
                    partial[f, 0] + zero[f, 1] + one[f, 1],
                    partial[f, 1] + zero[f, 2],
                ]
            )
            rows = silu(rows)
            spread(fs.at[f], 0, rows.astype(BF16), width)

    def no_far_edges():
        for f in range(local_frames):
            last = silu(partial[f, 1])
            rows = jnp.stack([jnp.zeros_like(last), jnp.zeros_like(last), last])
            spread(fs.at[f], 0, rows.astype(BF16), width)

    stage(far_edges, others)
    stage(no_far_edges, 1 - others)
    far_copies = second_half(0, 0)

    for copy in late_loads:
        copy.wait()
    span = frame_count * GROUP
    lane = lax.broadcasted_iota(jnp.int32, (frame_count, span), 1)
    wide = jnp.zeros((frame_count, span), F32)
    for g in range(frame_count):
        inside = (lane >= g * GROUP) & (lane < (g + 1) * GROUP)
        wide = jnp.where(inside, bias_ref[:, g : g + 1], wide)
    wide = jnp.broadcast_to(wide[:, None, :], (frame_count, GROUP, span)).reshape(span, span)
    query_pixel = jnp.bitwise_and(lax.broadcasted_iota(jnp.int32, (span, span), 0), GROUP - 1)
    key_pixel = jnp.bitwise_and(lax.broadcasted_iota(jnp.int32, (span, span), 1), GROUP - 1)
    masked_bias[...] = jnp.where(query_pixel == key_pixel, wide, -1e30)

    @stage
    def _():
        wide = lax.dot_general(
            wq[...], wk[...], (((1,), (1,)), ((), ())), preferred_element_type=F32
        )
        w_score[...] = (wide * (1.0 / math.sqrt(channels))).astype(BF16)
        w_mixed[...] = matmul(wv[...], wo[...]).astype(BF16)


    def attend(half, copies, cols_row):
        for copy in copies:
            copy.wait_recv()

        @stage
        def _():
            here = moved.at[half]
            groups = [slice(g * GROUP, (g + 1) * GROUP) for g in range(slots // GROUP)]
            residual, queries, values, scores = [], [], [], []
            for part in groups:
                taps = [
                    matmul(here[tap : tap + frame_count, part].reshape(span, channels), tk[tap])
                    for tap in range(3)
                ]
                centre = here[1 : 1 + frame_count, part].reshape(span, channels).astype(F32)
                residual.append((centre + taps[0] + taps[1] + taps[2]).astype(BF16).astype(F32))
            gained = [(widened * gain_ref[...]).astype(BF16) for widened in residual]
            for r in gained:
                queries.append(matmul(r, w_score[...]).astype(BF16))
            scales = [
                lax.rsqrt(jnp.mean(widened * widened, axis=-1, keepdims=True) + 1e-06)
                for widened in residual
            ]
            keys = [
                (widened * scale * gain_ref[...]).astype(BF16)
                for widened, scale in zip(residual, scales)
            ]
            for r, scale in zip(gained, scales):
                values.append((matmul(r, w_mixed[...]) * scale).astype(BF16))
            for q, k in zip(queries, keys):
                scores.append(
                    lax.dot_general(
                        q, k, (((1,), (1,)), ((), ())), preferred_element_type=F32
                    )
                )
            scores = [
                score * scale + masked_bias[...] for score, scale in zip(scores, scales)
            ]
            peaks = [jnp.max(score, axis=-1, keepdims=True) for score in scores]
            raised = [jnp.exp(score - peak) for score, peak in zip(scores, peaks)]
            totals = [1.0 / jnp.sum(r, axis=-1, keepdims=True) for r in raised]
            parts = []
            for r, t, v, w in zip(raised, totals, values, residual):
                mixed = w + matmul(r.astype(BF16), v) * t
                parts.append(mixed.reshape(frame_count, GROUP, channels))
            attended = jnp.concatenate(parts, axis=1)
            outer = attended[:, inner : inner + cols]
            place = lax.broadcasted_iota(jnp.int32, outer.shape, 1)
            for j in range(half_rows):
                here = attended[:, j * cols : (j + 1) * cols]
                edge_pair = pltpu.roll(outer, (cols - 1 - 2 * j) % cols, 1)
                left = pltpu.roll(jnp.where(place == cols - 1, edge_pair, here), 1, 1)
                right = pltpu.roll(jnp.where(place == 0, edge_pair, here), cols - 1, 1)
                for b, part in enumerate((left, here, right)):
                    cols3[cols_row + j, :, b * channels : (b + 1) * channels] = part.reshape(
                        frame_count * cols, channels
                    ).astype(BF16)

    def third(rows, a):
        part = matmul(rows.reshape(-1, 3 * channels), w3[mirrored(a, 3)].reshape(3 * channels, channels))
        return part.reshape(-1, frame_count, cols, channels)

    attend(1, near_copies, half_rows)
    for copy in w3_loads:
        copy.wait()

    def near_third():
        two = third(cols3[half_rows : n + 2], 2)
        one = third(cols3[half_rows : n + 1], 1)
        zero = third(cols3[half_rows:n], 0)
        partial3[0] = two[0]
        partial3[1] = two[1] + one[0]
        out_ref[:, mirrored(n - 1, n)] = (two[2] + one[1] + zero[0]).astype(BF16)

    def far_third():
        zero = third(cols3[0:half_rows], 0)
        one = third(cols3[1:half_rows], 1)
        two = third(cols3[2:half_rows], 2)
        out_ref[:, mirrored(0, n)] = (zero[0] + one[0] + two[0]).astype(BF16)
        out_ref[:, mirrored(1, n)] = (partial3[0] + zero[1] + one[1]).astype(BF16)
        out_ref[:, mirrored(2, n)] = (partial3[1] + zero[2]).astype(BF16)

    def whole_third():
        sums = [third(cols3[a : a + n], a) for a in range(3)]
        summed = sums[0] + sums[1] + sums[2]
        for t in range(n):
            out_ref[:, mirrored(t, n)] = summed[t].astype(BF16)

    stage(near_third, others)
    attend(0, far_copies, 0)
    stage(far_third, others)
    stage(whole_third, 1 - others)

    pl.when(has_far)(to_far.wait_send)
    to_near.wait_send()
    for copy in near_copies + far_copies:
        copy.wait_send()


def on_device(frames_axis, rows_axis, *args):
    frames_in = args[0]
    norm_gain = args[4]
    local_frames, n, width, channels = frames_in.shape
    frame_count = local_frames * frames_axis
    cols = width // frames_axis
    half_rows = (n + 2) // 2
    slots = -(-half_rows * (cols + 2) // GROUP) * GROUP
    args = args[:4] + (norm_gain.reshape(1, channels),) + args[5:]
    any_space = pl.BlockSpec(memory_space=pl.ANY)
    vmem = pl.BlockSpec(memory_space=pltpu.VMEM)
    weight = pltpu.VMEM((3, 3, channels, channels), BF16)
    square = pltpu.VMEM((channels, channels), BF16)
    halo = pltpu.VMEM((local_frames, HALO, width, channels), BF16)
    return pl.pallas_call(
        functools.partial(kernel, frames_axis, rows_axis),
        out_shape=pltpu.VMEM((frame_count, n, cols, channels), BF16),
        in_specs=[any_space] * 11,
        out_specs=vmem,
        scratch_shapes=[
            pltpu.VMEM((local_frames, n, width, channels), BF16),
            halo,
            halo,
            pltpu.VMEM((local_frames, n + 2 * HALO, width, 3 * channels), BF16),
            pltpu.VMEM((local_frames, n + 4, width, 3 * channels), BF16),
            weight,
            weight,
            pltpu.VMEM((3, channels, channels), BF16),
            square,
            square,
            square,
            square,
            weight,
            pltpu.VMEM((local_frames, 4, width, channels), F32),
            pltpu.VMEM((2, frame_count, cols, channels), F32),
            pltpu.VMEM((1, channels), F32),
            pltpu.VMEM((frame_count, frame_count), F32),
            pltpu.VMEM((2, frames_axis, local_frames, slots, channels), BF16),
            pltpu.VMEM((2, frame_count + 2, slots, channels), BF16),
            pltpu.VMEM((frame_count * GROUP, frame_count * GROUP), F32),
            square,
            square,
            pltpu.VMEM((n + 2, frame_count * cols, 3 * channels), BF16),
            pltpu.SemaphoreType.DMA((11,)),
            pltpu.SemaphoreType.REGULAR,
            pltpu.SemaphoreType.REGULAR,
            pltpu.SemaphoreType.REGULAR,
            pltpu.SemaphoreType.DMA((2,)),
            pltpu.SemaphoreType.DMA((2,)),
            pltpu.SemaphoreType.DMA((2, frames_axis)),
            pltpu.SemaphoreType.DMA((2, frames_axis)),
        ],
        compiler_params=pltpu.CompilerParams(
            collective_id=0, has_side_effects=True, vmem_limit_bytes=56 * 1024 * 1024
        ),
    )(*args)


def solution(mesh):
    placed = (P("frame", "row", None, None),) + (P(),) * 10
    return jax.shard_map(
        functools.partial(on_device, mesh.shape["frame"], mesh.shape["row"]),
        mesh=mesh,
        in_specs=placed,
        out_specs=P(None, "row", "frame", None),
        check_vma=False,
    )
```
